32 devices in a mesh: fsdp: 8 (over y, x, core), tp: 4 (over z).
Axes of the slice: x: 2, y: 2, z: 4, core: 2. Of those that a mesh axis runs over, the one named last changes fastest.
Arguments:
- tokens: bfloat16 [8192, 2048], P(('fsdp', 'tp')), may hold values from -6 to 6
- norm1_gain: float32 [2048], replicated, may hold values from 0.25 to 1.75
- norm1_shift: float32 [2048], replicated, may hold values from -1 to 1
- w_query: bfloat16 [2048, 2048], P('fsdp', 'tp'), may hold values from -0.125 to 0.125
- b_query: float32 [2048], P('tp'), may hold values from -1 to 1
- w_key: bfloat16 [2048, 2048], P('fsdp', 'tp'), may hold values from -0.125 to 0.125
- w_value: bfloat16 [2048, 2048], P('fsdp', 'tp'), may hold values from -0.125 to 0.125
- b_value: float32 [2048], P('tp'), may hold values from -1 to 1
- w_out: bfloat16 [2048, 2048], P('fsdp', 'tp'), may hold values from -0.5 to 0.5
- b_out: float32 [2048], replicated, may hold values from -1 to 1
- norm2_gain: float32 [2048], replicated, may hold values from 0.25 to 1.75
- norm2_shift: float32 [2048], replicated, may hold values from -1 to 1
- w_up: bfloat16 [2048, 8192], P('fsdp', 'tp'), may hold values from -0.125 to 0.125
- b_up: float32 [8192], P('tp'), may hold values from -1 to 1
- w_down: bfloat16 [2048, 8192], P('fsdp', 'tp'), may hold values from -0.09375 to 0.09375
- b_down: float32 [2048], replicated, may hold values from -1 to 1
- teacher: bfloat16 [8192, 2048], P(('fsdp', 'tp')), may hold values from -6 to 6
- valid_mask: int32 [8192], P(('fsdp', 'tp')), may hold values from 0 to 1, as said below
- parents: int32 [8, 8], P('fsdp'), may hold values from -1 to 6, as said below
- summary: int32 [8, 8, 12], P('fsdp'), may hold values from 0 to 127, as said below
Outputs:
- output_states: bfloat16 [8192, 2048], P(('fsdp', 'tp'))
- mean_loss: float32 [], replicated
- grad_tokens: float32 [8192, 2048], P(('fsdp', 'tp'))
- grad_norm1_gain: float32 [2048], replicated
- grad_norm1_shift: float32 [2048], replicated
- grad_w_query: float32 [2048, 2048], P('fsdp', 'tp')
- grad_b_query: float32 [2048], P('tp')
- grad_w_key: float32 [2048, 2048], P('fsdp', 'tp')
- grad_w_value: float32 [2048, 2048], P('fsdp', 'tp')
- grad_b_value: float32 [2048], P('tp')
- grad_w_out: float32 [2048, 2048], P('fsdp', 'tp')
- grad_b_out: float32 [2048], replicated
- grad_norm2_gain: float32 [2048], replicated
- grad_norm2_shift: float32 [2048], replicated
- grad_w_up: float32 [2048, 8192], P('fsdp', 'tp')
- grad_b_up: float32 [8192], P('tp')
- grad_w_down: float32 [2048, 8192], P('fsdp', 'tp')
- grad_b_down: float32 [2048], replicated
The draws below stay inside these ranges and needn't reach their ends.
Inputs may be any that keep to these rules, and one draw needn't show every extreme that they name: valid_mask is 1 at the first token of every tree. parents[f, 0] is -1 and 0 <= parents[f, s] < s for every later segment s; the last segment of every tree has the segment before it as parent. `summary`: the 12 offsets of one segment are distinct.
All inputs are finite; a program needn't handle non-finite values.
Results may differ from the reference program's by a relative error of at most 0.019.
Values may be sent and summed in bfloat16 or wider, within the bound.
No kernel may reach another device: no remote copies, remote signals or barrier semaphores. Data moves between devices by JAX's collectives and lax.ppermute only.
A program may use at most 192 MiB of HBM per device.

```python
import jax
import jax.numpy as jnp
from jax import lax

D = 2048
H = 32
HD = 64
FF = 8192
TOK_DEV = 1024
SEG = 128
SUMM = 12
NSEG = 8
TREES = 8
TOKENS = 8192


def draw_valid_mask(key, part):
    spots = jnp.arange(TREES * TOK_DEV, dtype=jnp.int32)
    tree_index = spots // TOK_DEV
    position = spots % TOK_DEV
    base_level = max(TREES - 1, 1)
    levels = jax.random.randint(key, (TREES * TOK_DEV,), 0, 4 * base_level)
    kept = jnp.where(levels < base_level + 2 * tree_index, 1, 0)
    return jnp.where(position == 0, 1, kept).astype(jnp.int32)


def draw_parents(key, part):
    upper = jnp.arange(NSEG, dtype=jnp.int32)
    raw_values = jax.random.randint(key, (TREES, NSEG), 0, 1 << 20)
    chosen = raw_values % jnp.maximum(upper, 1)[None, :]
    chosen = jnp.where(upper[None, :] == NSEG - 1, NSEG - 2, chosen)
    return jnp.where(upper[None, :] == 0, -1, chosen).astype(jnp.int32)


def draw_summary(key, part):
    raw_values = jax.random.randint(key, (TREES, NSEG, SEG), 0, 1 << 20)
    distinct = raw_values * SEG + jnp.arange(SEG, dtype=jnp.int32)[None, None, :]
    order = jnp.argsort(distinct, axis=-1)
    return order[:, :, :SUMM].astype(jnp.int32)


def block_levels(stream_key, shape, cuts, smallest, largest):
    loudness = 1.0
    for dim, blocks in cuts:
        steps = jax.random.uniform(jax.random.fold_in(jax.random.fold_in(stream_key, 6), dim), (blocks,), jnp.float32, smallest / len(cuts), largest / len(cuts))
        loudness = loudness * jnp.repeat(jnp.exp(steps), shape[dim] // blocks).reshape((-1,) + (1,) * (len(shape) - 1 - dim))
    return loudness


def normal_values(own_key, shape, scale, reach, pieces=(), kind=jnp.bfloat16):
    result = scale * jax.random.normal(own_key, shape, jnp.float32)
    if pieces:
        result = result * block_levels(own_key, shape, pieces, -0.22, 0.18)
    return jnp.clip(result, -reach, reach).astype(kind)


def setup_inputs(seed: int = 0) -> dict:
    streams_of = jax.random.split(jax.random.key(seed), 21)
    tokens = normal_values(streams_of[0], (TOKENS, D), 1.0, 6.0, ((0, 32),))
    norm1_gain = jnp.clip(1.0 + 0.15 * jax.random.normal(streams_of[1], (D,), jnp.float32), 0.25, 1.75)
    norm1_shift = normal_values(streams_of[2], (D,), 0.2, 1.0, (), jnp.float32)
    w_query = normal_values(streams_of[3], (D, D), D ** -0.5, 0.125, ((0, 8), (1, 4)))
    b_query = normal_values(streams_of[4], (D,), 0.2, 1.0, ((0, 4),), jnp.float32)
    w_key = normal_values(streams_of[5], (D, D), D ** -0.5, 0.125, ((0, 8), (1, 4)))
    w_value = normal_values(streams_of[6], (D, D), D ** -0.5, 0.125, ((0, 8), (1, 4)))
    b_value = normal_values(streams_of[7], (D,), 0.2, 1.0, ((0, 4),), jnp.float32)
    w_out = normal_values(streams_of[8], (D, D), (D // 16) ** -0.5, 0.5, ((0, 8), (1, 4)))
    b_out = normal_values(streams_of[9], (D,), 0.2, 1.0, (), jnp.float32)
    norm2_gain = jnp.clip(1.0 + 0.15 * jax.random.normal(streams_of[10], (D,), jnp.float32), 0.25, 1.75)
    norm2_shift = normal_values(streams_of[11], (D,), 0.2, 1.0, (), jnp.float32)
    w_up = normal_values(streams_of[12], (D, FF), D ** -0.5, 0.125, ((0, 8), (1, 4)))
    b_up = normal_values(streams_of[13], (FF,), 0.2, 1.0, ((0, 4),), jnp.float32)
    w_down = normal_values(streams_of[14], (D, FF), (FF // 2) ** -0.5, 0.09375, ((0, 8), (1, 4)))
    b_down = normal_values(streams_of[15], (D,), 0.2, 1.0, (), jnp.float32)
    teacher = normal_values(streams_of[16], (TOKENS, D), 1.0, 6.0, ((0, 32),))
    valid_mask = draw_valid_mask(jax.random.fold_in(streams_of[20], 71), 0)
    parents = draw_parents(jax.random.fold_in(streams_of[20], 71), 0)
    summary = draw_summary(jax.random.fold_in(streams_of[20], 71), 0)
    return {"tokens": tokens, "norm1_gain": norm1_gain, "norm1_shift": norm1_shift, "w_query": w_query, "b_query": b_query, "w_key": w_key, "w_value": w_value, "b_value": b_value, "w_out": w_out, "b_out": b_out, "norm2_gain": norm2_gain, "norm2_shift": norm2_shift, "w_up": w_up, "b_up": b_up, "w_down": w_down, "b_down": b_down, "teacher": teacher, "valid_mask": valid_mask, "parents": parents, "summary": summary}


@jax.custom_vjp
def low(v):
    return lax.optimization_barrier(v.astype(jnp.bfloat16)).astype(jnp.float32)

@jax.custom_vjp
def low_back(v):
    return v

def low_keep(v):
    return (low(v), None)

def low_pass(kept, grad):
    return (grad,)

def back_keep(v):
    return (v, None)

def back_low(kept, grad):
    return (low(grad),)
low.defvjp(low_keep, low_pass)
low_back.defvjp(back_keep, back_low)
EPSILON = 1e-05
MASKED_SCORE = -1e+30
HIGHEST_PRECISION = lax.Precision.HIGHEST

def layer_norm(vectors, norm_gain, norm_shift):
    centre = lax.optimization_barrier(jnp.mean(vectors, axis=-1, keepdims=True))
    centred = vectors - centre
    spread = lax.optimization_barrier(jnp.mean(centred * centred, axis=-1, keepdims=True))
    return centred * lax.rsqrt(spread + EPSILON) * norm_gain + norm_shift

def ancestors(parent_row):
    segments = parent_row.shape[0]
    columns = jnp.arange(segments, dtype=jnp.int32)

    def follow(sweep, state_pair):
        ancestry, current = state_pair
        matches = current[:, None] == columns[None, :]
        ancestry = jnp.maximum(ancestry, matches.astype(jnp.float32))
        following = lax.optimization_barrier(jnp.sum(jnp.where(matches, parent_row[None, :], 0), axis=1)).astype(jnp.int32)
        current = jnp.where(current >= 0, following, -1).astype(jnp.int32)
        return (ancestry, current)
    start_table = jnp.zeros((segments, segments), jnp.float32)
    ancestry, finished = lax.fori_loop(0, segments, follow, (start_table, parent_row.astype(jnp.int32)))
    return ancestry

def tree_tables(parent_row, summary_rows, length):
    segments = parent_row.shape[0]
    seg_length = length // segments
    ancestry = ancestors(parent_row)
    offsets = jnp.arange(seg_length, dtype=jnp.int32)
    marked = lax.optimization_barrier(jnp.max((summary_rows[:, :, None] == offsets[None, None, :]).astype(jnp.float32), axis=1)).reshape(length)
    key_segment = jnp.arange(length, dtype=jnp.int32) // seg_length
    key_onehot = (key_segment[:, None] == jnp.arange(segments, dtype=jnp.int32)[None, :]).astype(jnp.float32)
    return (ancestry, marked, key_segment, key_onehot, seg_length)

def block_mask(tables, start_row, block_rows, precision):
    ancestry, marked, key_segment, key_onehot, seg_length = tables
    query_position = start_row + jnp.arange(block_rows, dtype=jnp.int32)
    query_segment = query_position // seg_length
    query_onehot = (query_segment[:, None] == jnp.arange(ancestry.shape[0], dtype=jnp.int32)[None, :]).astype(jnp.float32)
    reached = jnp.dot(jnp.dot(query_onehot, ancestry, precision=precision), key_onehot.T, precision=precision)
    key_position = jnp.arange(marked.shape[0], dtype=jnp.int32)
    same_segment = (query_segment[:, None] == key_segment[None, :]) & (key_position[None, :] <= query_position[:, None])
    return same_segment | (reached > 0.5) & (marked[None, :] > 0.5)

def tree_attention(queries, key_states, value_states, parents, summary):
    block_rows = min(512, TOK_DEV)
    starts = jnp.arange(TOK_DEV // block_rows, dtype=jnp.int32) * block_rows

    def one_tree(members):
        query_heads, key_heads, value_heads, parent_row, summary_rows = members
        tables = tree_tables(parent_row, summary_rows, TOK_DEV)

        def one_block(start_row):
            query_block = lax.dynamic_slice_in_dim(query_heads, start_row, block_rows, 0)
            scores = low_back(jnp.einsum('qhd,khd->hqk', query_block, key_heads, precision=HIGHEST_PRECISION))
            allowed = block_mask(tables, start_row, block_rows, HIGHEST_PRECISION)
            scores = jnp.where(allowed[None], scores, MASKED_SCORE)
            shares = low(jax.nn.softmax(scores, axis=-1))
            return jnp.einsum('hqk,khd->qhd', shares, value_heads, precision=HIGHEST_PRECISION)
        return lax.map(jax.checkpoint(one_block), starts).reshape(TOK_DEV, H * HD)
    shape_four = (TREES, TOK_DEV, H, HD)
    attended = lax.map(jax.checkpoint(one_tree), (queries.reshape(shape_four), key_states.reshape(shape_four), value_states.reshape(shape_four), parents, summary))
    return attended.reshape(TREES * TOK_DEV, H * HD)

def forward(inputs, norm1_gain, norm1_shift, w_query, b_query, w_key, w_value, b_value, w_out, b_out, norm2_gain, norm2_shift, w_up, b_up, w_down, b_down, parents, summary):
    normed = low(layer_norm(inputs, norm1_gain, norm1_shift))
    queries = low_back(low((jnp.dot(normed, w_query, precision=HIGHEST_PRECISION) + b_query) * 0.125))
    key_states = low_back(low(jnp.dot(normed, w_key, precision=HIGHEST_PRECISION)))
    value_states = low_back(low(jnp.dot(normed, w_value, precision=HIGHEST_PRECISION) + b_value))
    attended = low_back(low(tree_attention(queries, key_states, value_states, parents, summary)))
    hidden = inputs + low_back(jnp.dot(attended, w_out.T, precision=HIGHEST_PRECISION)) + b_out
    normed_mid = low(layer_norm(hidden, norm2_gain, norm2_shift))
    active = low(jax.nn.relu(low_back(jnp.dot(normed_mid, w_up, precision=HIGHEST_PRECISION) + b_up)))
    return hidden + low_back(jnp.dot(active, w_down.T, precision=HIGHEST_PRECISION)) + b_down

def reference(tokens, norm1_gain, norm1_shift, w_query, b_query, w_key, w_value, b_value, w_out, b_out, norm2_gain, norm2_shift, w_up, b_up, w_down, b_down, teacher, valid_mask, parents, summary):
    floats = (tokens.astype(jnp.float32), norm1_gain, norm1_shift, w_query.astype(jnp.float32), b_query, w_key.astype(jnp.float32), w_value.astype(jnp.float32), b_value, w_out.astype(jnp.float32), b_out, norm2_gain, norm2_shift, w_up.astype(jnp.float32), b_up, w_down.astype(jnp.float32), b_down)

    def closed(*arrays):
        return forward(*arrays, parents, summary)
    output, pullback = jax.vjp(closed, *floats)
    weight_mask = valid_mask.astype(jnp.float32)
    valid_count = jnp.sum(weight_mask)
    deviation = output - teacher.astype(jnp.float32)
    mean_loss = jnp.sum(weight_mask[:, None] * deviation * deviation) / (valid_count * D)
    cotangent = 2.0 * TOKENS / valid_count * weight_mask[:, None] * deviation
    grads = pullback(cotangent)
    return (output.astype(jnp.bfloat16), mean_loss, grads[0], grads[1], grads[2], grads[3], grads[4], grads[5], grads[6], grads[7], grads[8], grads[9], grads[10], grads[11], grads[12], grads[13], grads[14], grads[15])
```

```python
import jax
import jax.numpy as jnp
from jax import lax
from jax.sharding import PartitionSpec as P

HD = 64


EPSILON = 1e-05
MASKED_SCORE = -1e30


def layer_norm(vectors, norm_gain, norm_shift):
    centre = jnp.mean(vectors, axis=-1, keepdims=True)
    centred = vectors - centre
    spread = jnp.mean(centred * centred, axis=-1, keepdims=True)
    return centred * lax.rsqrt(spread + EPSILON) * norm_gain + norm_shift


def ancestors(parent_row):
    segments = parent_row.shape[0]
    columns = jnp.arange(segments, dtype=jnp.int32)

    def follow(sweep, state_pair):
        ancestry, current = state_pair
        matches = current[:, None] == columns[None, :]
        ancestry = jnp.maximum(ancestry, matches.astype(jnp.float32))
        following = jnp.sum(jnp.where(matches, parent_row[None, :], 0), axis=1)
        current = jnp.where(current >= 0, following, -1)
        return (ancestry, current)

    start_table = jnp.zeros((segments, segments), jnp.float32)
    ancestry, finished = lax.fori_loop(0, segments, follow, (start_table, parent_row))
    return ancestry


def tree_tables(parent_row, summary_rows, length):
    segments = parent_row.shape[0]
    seg_length = length // segments
    ancestry = ancestors(parent_row)
    offsets = jnp.arange(seg_length, dtype=jnp.int32)
    marked = jnp.max(
        (summary_rows[:, :, None] == offsets[None, None, :]).astype(jnp.float32), axis=1
    ).reshape(length)
    key_segment = jnp.arange(length, dtype=jnp.int32) // seg_length
    key_onehot = (key_segment[:, None] == jnp.arange(segments, dtype=jnp.int32)[None, :]).astype(
        jnp.float32
    )
    return (ancestry, marked, key_segment, key_onehot, seg_length)


def block_mask(tables, start_row, block_rows):
    ancestry, marked, key_segment, key_onehot, seg_length = tables
    query_position = start_row + jnp.arange(block_rows, dtype=jnp.int32)
    query_segment = query_position // seg_length
    query_onehot = (
        query_segment[:, None] == jnp.arange(ancestry.shape[0], dtype=jnp.int32)[None, :]
    ).astype(jnp.float32)
    reached = jnp.dot(jnp.dot(query_onehot, ancestry, precision=None), key_onehot.T, precision=None)
    key_position = jnp.arange(marked.shape[0], dtype=jnp.int32)
    same_segment = (query_segment[:, None] == key_segment[None, :]) & (
        key_position[None, :] <= query_position[:, None]
    )
    return same_segment | (reached > 0.5) & (marked[None, :] > 0.5)


def contract(left_side, right_side, left_dim, right_dim):
    return lax.dot_general(
        left_side,
        right_side,
        (((left_dim,), (right_dim,)), ((), ())),
        preferred_element_type=jnp.float32,
    )


def attend_forward(queries, key_states, value_states, tables):
    length = queries.shape[0]
    head_count = queries.shape[1] // HD
    block_rows = min(512, length)
    query_heads = queries.reshape(length, head_count, HD)
    key_heads = key_states.reshape(length, head_count, HD)
    value_heads = value_states.reshape(length, head_count, HD)

    def one_block(start_row):
        query_block = lax.dynamic_slice_in_dim(query_heads, start_row, block_rows, 0)
        scores = jnp.einsum(
            "qhd,khd->hqk", query_block, key_heads, preferred_element_type=jnp.float32
        )
        allowed = block_mask(tables, start_row, block_rows)
        scores = jnp.where(allowed[None], scores, MASKED_SCORE)
        highest = jnp.max(scores, axis=-1, keepdims=True)
        exp_scores = jnp.exp(scores - highest)
        totals = jnp.sum(exp_scores, axis=-1, keepdims=True)
        shares = (exp_scores / totals).astype(jnp.bfloat16)
        attended = jnp.einsum(
            "hqk,khd->qhd", shares, value_heads, preferred_element_type=jnp.float32
        )
        return (attended.astype(jnp.bfloat16), (highest + jnp.log(totals))[..., 0])

    starts = jnp.arange(length // block_rows, dtype=jnp.int32) * block_rows
    attended, log_totals = lax.map(one_block, starts)
    return (attended.reshape(length, head_count * HD), log_totals)


def attend_backward(queries, key_states, value_states, grad_attended, log_totals, tables):
    length = queries.shape[0]
    head_count = queries.shape[1] // HD
    block_rows = min(512, length)
    query_heads = queries.reshape(length, head_count, HD)
    key_heads = key_states.reshape(length, head_count, HD)
    value_heads = value_states.reshape(length, head_count, HD)
    grad_heads = grad_attended.reshape(length, head_count, HD)

    def one_block(summed, members):
        start_row, log_block = members
        key_sum, value_sum = summed
        query_block = lax.dynamic_slice_in_dim(query_heads, start_row, block_rows, 0)
        grad_block = lax.dynamic_slice_in_dim(grad_heads, start_row, block_rows, 0)
        scores = jnp.einsum(
            "qhd,khd->hqk", query_block, key_heads, preferred_element_type=jnp.float32
        )
        allowed = block_mask(tables, start_row, block_rows)
        probs = jnp.where(allowed[None], jnp.exp(scores - log_block[..., None]), 0.0)
        grad_probs = jnp.einsum(
            "qhd,khd->hqk", grad_block, value_heads, preferred_element_type=jnp.float32
        )
        inner_sum = jnp.sum(probs * grad_probs, axis=-1, keepdims=True)
        grad_scores = (probs * (grad_probs - inner_sum)).astype(jnp.bfloat16)
        grad_query = jnp.einsum(
            "hqk,khd->qhd", grad_scores, key_heads, preferred_element_type=jnp.float32
        ).astype(jnp.bfloat16)
        key_sum = key_sum + jnp.einsum(
            "hqk,qhd->khd", grad_scores, query_block, preferred_element_type=jnp.float32
        )
        value_sum = value_sum + jnp.einsum(
            "hqk,qhd->khd",
            probs.astype(jnp.bfloat16),
            grad_block,
            preferred_element_type=jnp.float32,
        )
        return ((key_sum, value_sum), grad_query)

    starts = jnp.arange(length // block_rows, dtype=jnp.int32) * block_rows
    zero_heads = jnp.zeros((length, head_count, HD), jnp.float32)
    (key_sum, value_sum), grad_queries = lax.scan(
        one_block, (zero_heads, zero_heads), (starts, log_totals)
    )
    width = head_count * HD
    return (
        grad_queries.reshape(length, width),
        key_sum.reshape(length, width).astype(jnp.bfloat16),
        value_sum.reshape(length, width).astype(jnp.bfloat16),
    )


def scatter_narrow(partial_sums, axis):
    narrow_sums = lax.psum_scatter(
        partial_sums.astype(jnp.bfloat16), axis, scatter_dimension=0, tiled=True
    )
    return narrow_sums.astype(jnp.float32)


def body(
    tokens,
    norm1_gain,
    norm1_shift,
    w_query,
    b_query,
    w_key,
    w_value,
    b_value,
    w_out,
    b_out,
    norm2_gain,
    norm2_shift,
    w_up,
    b_up,
    w_down,
    b_down,
    teacher,
    valid_mask,
    parents,
    summary,
):

    def attention_weights():
        return (
            lax.all_gather(w_query, "fsdp", axis=0, tiled=True),
            lax.all_gather(w_key, "fsdp", axis=0, tiled=True),
            lax.all_gather(w_value, "fsdp", axis=0, tiled=True),
            lax.all_gather(w_out, "fsdp", axis=0, tiled=True),
        )

    def feed_weights():
        return (
            lax.all_gather(w_up, "fsdp", axis=0, tiled=True),
            lax.all_gather(w_down, "fsdp", axis=0, tiled=True),
        )

    inputs = tokens.astype(jnp.float32)
    normed = layer_norm(inputs, norm1_gain, norm1_shift).astype(jnp.bfloat16)
    normed_all = lax.all_gather(normed, "tp", axis=0, tiled=True)
    full_query, full_key, full_value, full_out = attention_weights()
    queries = (
        (jnp.dot(normed_all, full_query, preferred_element_type=jnp.float32) + b_query) * 0.125
    ).astype(jnp.bfloat16)
    key_states = jnp.dot(normed_all, full_key, preferred_element_type=jnp.float32).astype(
        jnp.bfloat16
    )
    value_states = (
        jnp.dot(normed_all, full_value, preferred_element_type=jnp.float32) + b_value
    ).astype(jnp.bfloat16)
    tables = tree_tables(parents[0], summary[0], normed_all.shape[0])
    attended, log_totals = attend_forward(queries, key_states, value_states, tables)
    branch = scatter_narrow(contract(attended, full_out, 1, 1), "tp")
    hidden = inputs + branch + b_out
    normed_mid = layer_norm(hidden, norm2_gain, norm2_shift).astype(jnp.bfloat16)
    normed_mid_all = lax.all_gather(normed_mid, "tp", axis=0, tiled=True)
    full_up, full_down = feed_weights()
    active = jnp.maximum(
        jnp.dot(normed_mid_all, full_up, preferred_element_type=jnp.float32) + b_up, 0.0
    ).astype(jnp.bfloat16)
    feed_out = scatter_narrow(contract(active, full_down, 1, 1), "tp")
    output = hidden + feed_out + b_down
    weight_mask = valid_mask.astype(jnp.float32)
    deviation = output - teacher.astype(jnp.float32)
    valid_count, squares = lax.psum(
        (jnp.sum(weight_mask), jnp.sum(weight_mask[:, None] * deviation * deviation)),
        ("fsdp", "tp"),
    )
    mean_loss = squares / (valid_count * tokens.shape[1])
    total_tokens = tokens.shape[0] * lax.axis_size("fsdp") * lax.axis_size("tp")
    grad_output = 2.0 * total_tokens / valid_count * weight_mask[:, None] * deviation
    grad_feed_all = lax.all_gather(grad_output.astype(jnp.bfloat16), "tp", axis=0, tiled=True)
    full_up, full_down = feed_weights()
    grad_w_down = contract(grad_feed_all, active, 0, 0)
    grad_pre = jnp.where(
        active > 0, jnp.dot(grad_feed_all, full_down, preferred_element_type=jnp.float32), 0.0
    ).astype(jnp.bfloat16)
    grad_w_up = contract(normed_mid_all, grad_pre, 0, 0)
    grad_w_up, grad_w_down = (
        lax.psum_scatter(
            grad_w_up.astype(jnp.bfloat16), "fsdp", scatter_dimension=0, tiled=True
        ).astype(jnp.float32),
        lax.psum_scatter(
            grad_w_down.astype(jnp.bfloat16), "fsdp", scatter_dimension=0, tiled=True
        ).astype(jnp.float32),
    )
    grad_mid = scatter_narrow(contract(grad_pre, full_up, 1, 1), "tp")
    second_norm, second_pull = jax.vjp(layer_norm, hidden, norm2_gain, norm2_shift)
    grad_hidden_norm, grad_norm2_gain, grad_norm2_shift = second_pull(grad_mid)
    grad_hidden = grad_output + grad_hidden_norm
    grad_branch_all = lax.all_gather(grad_hidden.astype(jnp.bfloat16), "tp", axis=0, tiled=True)
    full_query, full_key, full_value, full_out = attention_weights()
    grad_w_out = contract(grad_branch_all, attended, 0, 0)
    grad_attended = jnp.dot(grad_branch_all, full_out, preferred_element_type=jnp.float32).astype(
        jnp.bfloat16
    )
    grad_queries, grad_keys, grad_values = attend_backward(
        queries, key_states, value_states, grad_attended, log_totals, tables
    )
    grad_pre_query = grad_queries * jnp.bfloat16(0.125)
    grad_w_query = contract(normed_all, grad_pre_query, 0, 0)
    grad_w_key = contract(normed_all, grad_keys, 0, 0)
    grad_w_value = contract(normed_all, grad_values, 0, 0)
    grad_w_query, grad_w_key, grad_w_value, grad_w_out = (
        scatter_narrow(grad_w_query, "fsdp"),
        scatter_narrow(grad_w_key, "fsdp"),
        scatter_narrow(grad_w_value, "fsdp"),
        scatter_narrow(grad_w_out, "fsdp"),
    )
    grad_normed = (
        contract(grad_pre_query, full_query, 1, 1)
        + contract(grad_keys, full_key, 1, 1)
        + contract(grad_values, full_value, 1, 1)
    )
    grad_normed = scatter_narrow(grad_normed, "tp")
    first_norm, first_pull = jax.vjp(layer_norm, inputs, norm1_gain, norm1_shift)
    grad_input_norm, grad_norm1_gain, grad_norm1_shift = first_pull(grad_normed)
    grad_tokens = grad_hidden + grad_input_norm
    column = lax.axis_index("tp")
    tp_count = lax.axis_size("tp")

    def widen(share_part):
        widened = jnp.zeros((share_part.shape[0] * tp_count,), jnp.float32)
        return lax.dynamic_update_slice_in_dim(widened, share_part, column * share_part.shape[0], 0)

    def narrow(widened, span_width):
        return lax.dynamic_slice_in_dim(widened, column * span_width, span_width, 0)

    summed = lax.psum(
        (
            grad_norm1_gain,
            grad_norm1_shift,
            widen(jnp.sum(grad_pre_query.astype(jnp.float32), axis=0)),
            widen(jnp.sum(grad_values.astype(jnp.float32), axis=0)),
            jnp.sum(grad_hidden, axis=0),
            grad_norm2_gain,
            grad_norm2_shift,
            widen(jnp.sum(grad_pre.astype(jnp.float32), axis=0)),
            jnp.sum(grad_output, axis=0),
        ),
        ("fsdp", "tp"),
    )
    return (
        output.astype(jnp.bfloat16),
        mean_loss,
        grad_tokens,
        summed[0],
        summed[1],
        grad_w_query,
        narrow(summed[2], b_query.shape[0]),
        grad_w_key,
        grad_w_value,
        narrow(summed[3], b_value.shape[0]),
        grad_w_out,
        summed[4],
        summed[5],
        summed[6],
        grad_w_up,
        narrow(summed[7], b_up.shape[0]),
        grad_w_down,
        summed[8],
    )


def solution(mesh):
    placed = (
        P(("fsdp", "tp"), None),
        P(),
        P(),
        P("fsdp", "tp"),
        P("tp"),
        P("fsdp", "tp"),
        P("fsdp", "tp"),
        P("tp"),
        P("fsdp", "tp"),
        P(),
        P(),
        P(),
        P("fsdp", "tp"),
        P("tp"),
        P("fsdp", "tp"),
        P(),
        P(("fsdp", "tp"), None),
        P(("fsdp", "tp")),
        P("fsdp", None),
        P("fsdp", None, None),
    )
    return jax.shard_map(
        body,
        mesh=mesh,
        in_specs=placed,
        out_specs=(
            P(("fsdp", "tp"), None),
            P(),
            P(("fsdp", "tp"), None),
            P(),
            P(),
            P("fsdp", "tp"),
            P("tp"),
            P("fsdp", "tp"),
            P("fsdp", "tp"),
            P("tp"),
            P("fsdp", "tp"),
            P(),
            P(),
            P(),
            P("fsdp", "tp"),
            P("tp"),
            P("fsdp", "tp"),
            P(),
        ),
        check_vma=False,
    )
```

```python
import jax
import jax.numpy as jnp
from jax import lax
from jax.experimental import pallas as pl
from jax.experimental.pallas import tpu as pltpu
from jax.sharding import PartitionSpec as P

HD = 64
PAIR = 2 * HD
EPSILON = 1e-05
MASKED_SCORE = -1e30
KEY_PAD = 128


def layer_norm(vectors, norm_gain, norm_shift):
    centre = jnp.mean(vectors, axis=-1, keepdims=True)
    centred = vectors - centre
    spread = jnp.mean(centred * centred, axis=-1, keepdims=True)
    return centred * lax.rsqrt(spread + EPSILON) * norm_gain + norm_shift


def contract(left_side, right_side, left_dim, right_dim):
    return lax.dot_general(
        left_side,
        right_side,
        (((left_dim,), (right_dim,)), ((), ())),
        preferred_element_type=jnp.float32,
    )


def narrow(values):
    return values.astype(jnp.bfloat16)


def bits_below(count, first):
    bits = []
    bit = first
    while bit < count:
        bits.append(bit)
        bit *= 2
    return bits


def segment_scores(q_ref, k_ref, ks_ref, seen_ref, row, seg, tree, place):
    rows = pl.ds(row, seg)
    lane = lax.broadcasted_iota(jnp.int32, (seg, PAIR), 1)
    first_head = lane < HD
    query = q_ref[rows, :]
    none = jnp.zeros_like(query)
    both = jnp.concatenate(
        [jnp.where(first_head, query, none), jnp.where(first_head, none, query)], axis=0
    )
    keys = jnp.concatenate([k_ref[rows, :], ks_ref[tree]], axis=0)
    scores = contract(both, keys, 1, 1)
    width = seg + KEY_PAD
    column = lax.broadcasted_iota(jnp.int32, (2 * seg, width), 1)
    position = lax.broadcasted_iota(jnp.int32, (2 * seg, width), 0)
    position = jnp.where(position >= seg, position - seg, position)
    seen = jnp.concatenate(
        [jnp.ones((1, seg), jnp.float32), seen_ref[pl.ds(place, 1), :]], axis=1
    )
    reach = jnp.where(column < seg, position, width)
    allowed = (column <= reach) & (seen > 0.5)
    scores = jnp.where(allowed, scores, MASKED_SCORE)
    highest = jnp.max(scores, axis=1, keepdims=True)
    raised = jnp.exp(scores - highest)
    probs = raised * (1.0 / jnp.sum(raised, axis=1, keepdims=True))
    return rows, first_head, both, keys, probs


def walk_segments(blocks, rows, seg, step):
    per = rows // seg
    for block in range(blocks):
        tree, far = block % 2, block // 2
        for inner in range(per):
            step(block * rows + inner * seg, tree, (tree * 2 + far) * per + inner)


def forward_kernel(rows, seg, q_ref, k_ref, v_ref, ks_ref, vs_ref, seen_ref, out_ref):
    def step(row, tree, place):
        at, first_head, both, keys, probs = segment_scores(
            q_ref, k_ref, ks_ref, seen_ref, row, seg, tree, place
        )
        values = jnp.concatenate([v_ref[at, :], vs_ref[tree]], axis=0)
        mixed = contract(narrow(probs), values, 1, 0)
        out_ref[at, :] = narrow(jnp.where(first_head, mixed[:seg], mixed[seg:]))

    walk_segments(4, rows, seg, step)


def backward_kernel(
    rows, seg, q_ref, k_ref, v_ref, go_ref, ks_ref, vs_ref, seen_ref, gq_ref, gk_ref, gv_ref, gks_ref, gvs_ref
):
    gks_ref[...] = jnp.zeros_like(gks_ref)
    gvs_ref[...] = jnp.zeros_like(gvs_ref)

    def step(row, tree, place):
        at, first_head, both, keys, probs = segment_scores(
            q_ref, k_ref, ks_ref, seen_ref, row, seg, tree, place
        )
        values = jnp.concatenate([v_ref[at, :], vs_ref[tree]], axis=0)
        grad_out = go_ref[at, :]
        none = jnp.zeros_like(grad_out)
        grad_both = jnp.concatenate(
            [jnp.where(first_head, grad_out, none), jnp.where(first_head, none, grad_out)], axis=0
        )
        grad_probs = contract(grad_both, values, 1, 1)
        inner = jnp.sum(probs * grad_probs, axis=1, keepdims=True)
        grad_scores = narrow(probs * (grad_probs - inner))
        grad_query = contract(grad_scores, keys, 1, 0)
        grad_query = narrow(jnp.where(first_head, grad_query[:seg], grad_query[seg:]))
        gq_ref[at, :] = grad_query * jnp.bfloat16(0.125)
        grad_keys = contract(grad_scores, both, 0, 0)
        gk_ref[at, :] = narrow(grad_keys[:seg])
        gks_ref[tree] += grad_keys[seg:]
        grad_values = contract(narrow(probs), grad_both, 0, 0)
        gv_ref[at, :] = narrow(grad_values[:seg])
        gvs_ref[tree] += grad_values[seg:]

    walk_segments(4, rows, seg, step)


def attend(kernel, rows, seg, operands, key_sums, seen, outputs, sums):
    count, width = operands[0].shape
    column_block = pl.BlockSpec((count, PAIR), lambda pair: (0, pair))
    sum_block = pl.BlockSpec((2, KEY_PAD, PAIR), lambda pair: (0, 0, pair))
    return pl.pallas_call(
        lambda *refs: kernel(rows, seg, *refs),
        grid=(width // PAIR,),
        in_specs=[column_block] * len(operands)
        + [sum_block] * 2
        + [pl.BlockSpec(seen.shape, lambda pair: (0, 0))],
        out_specs=[column_block] * outputs + [sum_block] * sums,
        out_shape=[jax.ShapeDtypeStruct((count, width), jnp.bfloat16)] * outputs
        + [jax.ShapeDtypeStruct((2, KEY_PAD, width), jnp.float32)] * sums,
        name="attend_forward" if sums == 0 else "attend_backward",
    )(*operands, *key_sums, seen)


def make_body(fsdp, tp):
    world = fsdp * tp
    low = 1
    top = tp // 2
    middle = bits_below(top, 2)
    mate = tp
    plane = bits_below(world, 2 * tp)

    def swap(values, mask):
        return lax.ppermute(values, ("fsdp", "tp"), [(i, i ^ mask) for i in range(world)])

    def agrees(i):
        return (i // tp) % 2 == (i % tp) // top

    def send(values, mask, alike):
        pairs = [(i, i ^ mask) for i in range(world) if agrees(i) == alike]
        return lax.ppermute(values, ("fsdp", "tp"), pairs)

    def everyone(values):
        for mask in bits_below(world, 1):
            values = values + swap(values, mask)
        return values

    def body(
        tokens,
        norm1_gain,
        norm1_shift,
        w_query,
        b_query,
        w_key,
        w_value,
        b_value,
        w_out,
        b_out,
        norm2_gain,
        norm2_shift,
        w_up,
        b_up,
        w_down,
        b_down,
        teacher,
        valid_mask,
        parents,
        summary,
    ):
        rows, depth = tokens.shape
        strip = depth // fsdp
        half = depth // 2
        column = lax.axis_index("tp")
        device = lax.axis_index("fsdp")
        core = device % 2
        spot = device // 2
        upper = column // top
        alike = core == upper
        segments = parents.shape[1]
        marks = summary.shape[2]
        seg = rows * tp // segments
        per = rows // seg

        def mirrored(k):
            mirror, found = 0, 0
            for i in range(len(plane)):
                found = (k >> i) & 1
                mirror = mirror * 2 + found
            return mirror

        blocks = fsdp // 2

        def to_relative(values):
            parts = []
            for side in range(2):
                for k in range(blocks):
                    away = k if side == 0 else mirrored(k)
                    start = (2 * (spot ^ away) + side) * strip
                    parts.append(lax.dynamic_slice_in_dim(values, start, strip, values.ndim - 1))
            return jnp.concatenate(parts, axis=-1)

        def to_absolute(values):
            parts = []
            for place in range(blocks):
                away = spot ^ place
                back = jnp.zeros_like(away)
                for i in range(len(plane)):
                    back = back * 2 + ((away >> i) & 1)
                for side in range(2):
                    start = (away if side == 0 else blocks + back) * strip
                    parts.append(lax.dynamic_slice_in_dim(values, start, strip, values.ndim - 1))
            return jnp.concatenate(parts, axis=-1)

        def gather_weight(shard):
            near = send(shard, mate, False)
            far_same = send(shard, top, True)
            far_other = send(shard, mate | top, False)
            same = jnp.where(alike, shard, far_same)
            other = jnp.where(alike, near, far_other)
            for mask in middle:
                same = jnp.concatenate([same, swap(same, mask)], axis=1)
                other = jnp.concatenate([other, swap(other, mask)], axis=1)
            pieces = []
            for side, order in enumerate((plane, plane[::-1])):
                held = [jnp.where(core == side, same, other)]
                for mask in order:
                    now = held[0] if len(held) == 1 else jnp.concatenate(held, axis=0)
                    held.append(swap(now, mask))
                pieces += held
            return jnp.concatenate(pieces, axis=0)

        def scatter_weight(left, right):
            outs = []
            firsts = []
            for side, order in enumerate((plane, plane[::-1])):
                base = side * half
                away = narrow(contract(left[:, base + half // 2 : base + half], right, 0, 0))
                firsts.append((base, order, swap(away, order[-1])))
            for base, order, came in firsts:
                kept = contract(left[:, base : base + half // 2], right, 0, 0) + came
                for mask in order[-2::-1]:
                    size = kept.shape[0] // 2
                    kept = kept[:size] + swap(narrow(kept[size:]), mask)
                outs.append(kept)
            same = narrow(jnp.where(core == 0, outs[0], outs[1]))
            other = narrow(jnp.where(core == 0, outs[1], outs[0]))
            for mask in middle[::-1]:
                size = same.shape[1] // 2
                same = narrow(same[:, :size].astype(jnp.float32) + swap(same[:, size:], mask))
                other = narrow(other[:, :size].astype(jnp.float32) + swap(other[:, size:], mask))
            near = send(other, mate, True)
            far_same = send(same, top, False)
            far_other = send(other, mate | top, False)
            own = jnp.where(alike, same, jnp.zeros_like(same)).astype(jnp.float32)
            return own + near + far_same + far_other

        def gather_bias(part):
            part = jnp.where(alike, part, swap(part, top))
            for mask in middle:
                part = jnp.concatenate([part, swap(part, mask)], axis=1)
            return part

        def spread_rows(own):
            across = swap(own, low)
            near = jnp.concatenate([own, swap(own, mate)], axis=0)
            far = jnp.concatenate([across, swap(across, mate)], axis=0)
            return near, far

        def collect_rows(partial):
            far_mate = swap(narrow(partial(3)), mate)
            crossing = swap(narrow(partial(2) + far_mate), low)
            near_mate = swap(narrow(partial(1)), mate)
            return partial(0) + near_mate + crossing

        def row_block(values, block):
            return values[block * rows : (block + 1) * rows]

        inputs = to_relative(tokens).astype(jnp.float32)
        target = to_relative(teacher).astype(jnp.float32)
        vectors = to_relative(
            jnp.stack([norm1_gain, norm1_shift, b_out, norm2_gain, norm2_shift, b_down])
        )
        gain1, shift1, bias_out, gain2, shift2, bias_down = [vectors[i] for i in range(6)]
        weight_mask = valid_mask.astype(jnp.float32)[:, None]
        counted = everyone(jnp.full((8, 128), jnp.sum(weight_mask), jnp.float32))
        valid_count = counted[0, 0]

        slices = tp // 4
        w_kv = gather_weight(jnp.concatenate([w_key, w_value], axis=1))
        w_qo = gather_weight(jnp.concatenate([w_query, w_out], axis=1))
        full_up = gather_weight(w_up)
        full_down = gather_weight(w_down)

        def split_two(joined):
            parts = joined.reshape(joined.shape[0], slices, 2, -1)
            return [parts[:, :, i].reshape(joined.shape[0], -1) for i in range(2)]

        full_key, full_value = split_two(w_kv)
        full_query, full_out = split_two(w_qo)
        head_bias = gather_bias(jnp.stack([b_query, b_value]))
        bias_query, bias_value = head_bias[0], head_bias[1]
        bias_up = gather_bias(b_up[None])[0]

        tables = jnp.concatenate([parents[0][:, None], summary[0]], axis=1)
        tables = jnp.stack([tables, swap(tables, mate)])
        seg_ids = jnp.arange(segments, dtype=jnp.int32)
        moved = seg_ids ^ (column * per)
        picks = moved[:, None] == seg_ids[None, :]
        tables = jnp.sum(jnp.where(picks[None, :, :, None], tables[:, None], 0), axis=2)
        parent_rel = jnp.where(tables[:, :, 0] >= 0, tables[:, :, 0] ^ (column * per), -1)
        offsets_rel = tables[:, :, 1:]
        reach = (parent_rel[:, :, None] == seg_ids[None, None, :]).astype(jnp.float32)
        unit = (seg_ids[:, None] == seg_ids[None, :]).astype(jnp.float32)[None]
        closure = reach + unit
        steps = 1
        while steps < segments:
            closure = jnp.einsum("tij,tjk->tik", closure, closure)
            closure = jnp.minimum(closure, 1.0)
            steps *= 2
        closure = closure - unit
        local = 2 * per
        seen = jnp.repeat(closure[:, :local], marks, axis=2)
        seen = jnp.pad(seen, ((0, 0), (0, 0), (0, KEY_PAD - segments * marks)))
        seen = seen.reshape(2 * local, KEY_PAD)
        far_id = jnp.arange(local, dtype=jnp.int32) // per
        inner_id = jnp.arange(local, dtype=jnp.int32) % per
        tree_id = jnp.arange(2, dtype=jnp.int32)
        start = (far_id[None, :] * 2 + tree_id[:, None]) * rows + inner_id[None, :] * seg
        summary_row = (start[:, :, None] + offsets_rel[:, :local]).reshape(-1)
        chosen = narrow(summary_row[:, None] == jnp.arange(4 * rows, dtype=jnp.int32)[None, :])

        def spread_sums(part):
            for mask in middle + [top]:
                part = jnp.concatenate([part, swap(part, mask)], axis=1)
            return jnp.pad(part, ((0, 0), (0, KEY_PAD - part.shape[1]), (0, 0)))

        def collect_sums(whole):
            whole = whole[:, : segments * marks]
            for mask in [top] + middle[::-1]:
                size = whole.shape[1] // 2
                whole = whole[:, :size] + swap(narrow(whole[:, size:]), mask)
            return whole

        normed = narrow(layer_norm(inputs, gain1, shift1))
        normed_near, normed_far = spread_rows(normed)
        normed_all = jnp.concatenate([normed_near, normed_far], axis=0)
        key_states = narrow(contract(normed_all, full_key, 1, 0))
        value_states = narrow(contract(normed_all, full_value, 1, 0) + bias_value)
        queries = narrow((contract(normed_all, full_query, 1, 0) + bias_query) * 0.125)
        width = queries.shape[1]
        picked = jnp.concatenate(
            [narrow(contract(chosen, key_states, 1, 0)), narrow(contract(chosen, value_states, 1, 0))],
            axis=1,
        )
        picked = spread_sums(picked.reshape(2, local * marks, 2 * width))
        key_sums = (picked[:, :, :width], picked[:, :, width:])
        (attended,) = attend(
            forward_kernel, rows, seg, (queries, key_states, value_states), key_sums, seen, 1, 0
        )
        branch = collect_rows(lambda b: contract(row_block(attended, b), full_out, 1, 1))
        hidden = inputs + branch + bias_out

        normed_mid = narrow(layer_norm(hidden, gain2, shift2))
        mid_near, mid_far = spread_rows(normed_mid)
        active = [
            narrow(jnp.maximum(contract(part, full_up, 1, 0) + bias_up, 0.0))
            for part in (mid_near, mid_far)
        ]
        active_all = jnp.concatenate(active, axis=0)
        mid_all = jnp.concatenate([mid_near, mid_far], axis=0)
        feed_out = collect_rows(lambda b: contract(row_block(active_all, b), full_down, 1, 1))
        output = hidden + feed_out + bias_down

        deviation = output - target
        squares = jnp.sum(weight_mask * deviation * deviation)
        total_tokens = rows * world
        grad_output = (2.0 * total_tokens / valid_count) * weight_mask * deviation

        feed_near, feed_far = spread_rows(narrow(grad_output))
        feed_all = jnp.concatenate([feed_near, feed_far], axis=0)
        grad_pre = [
            narrow(jnp.where(kept > 0, contract(part, full_down, 1, 0), 0.0))
            for part, kept in zip((feed_near, feed_far), active)
        ]
        grad_pre_all = jnp.concatenate(grad_pre, axis=0)
        grad_mid = collect_rows(lambda b: contract(row_block(grad_pre_all, b), full_up, 1, 1))
        grad_w_down = scatter_weight(feed_all, active_all)
        grad_w_up = scatter_weight(mid_all, grad_pre_all)
        second_norm, second_pull = jax.vjp(layer_norm, hidden, gain2, shift2)
        grad_hidden_norm, grad_gain2, grad_shift2 = second_pull(grad_mid)
        grad_hidden = grad_output + grad_hidden_norm

        branch_near, branch_far = spread_rows(narrow(grad_hidden))
        branch_all = jnp.concatenate([branch_near, branch_far], axis=0)
        grad_attended = narrow(contract(branch_all, full_out, 1, 0))
        grad_w_out = scatter_weight(branch_all, attended)
        grad_pre_query, grad_keys, grad_values, key_part, value_part = attend(
            backward_kernel,
            rows,
            seg,
            (queries, key_states, value_states, grad_attended),
            key_sums,
            seen,
            3,
            2,
        )
        grad_w_query = scatter_weight(normed_all, grad_pre_query)
        parts = collect_sums(jnp.concatenate([key_part, value_part], axis=2))
        parts = narrow(parts.reshape(-1, 2 * width))
        grad_keys = narrow(grad_keys + contract(chosen, parts[:, :width], 0, 0))
        grad_values = narrow(grad_values + contract(chosen, parts[:, width:], 0, 0))
        grad_w_key = scatter_weight(normed_all, grad_keys)
        grad_w_value = scatter_weight(normed_all, grad_values)
        grad_normed = collect_rows(
            lambda b: contract(row_block(grad_pre_query, b), full_query, 1, 1)
            + contract(row_block(grad_keys, b), full_key, 1, 1)
            + contract(row_block(grad_values, b), full_value, 1, 1)
        )
        first_norm, first_pull = jax.vjp(layer_norm, inputs, gain1, shift1)
        grad_input_norm, grad_gain1, grad_shift1 = first_pull(grad_normed)
        grad_tokens = grad_hidden + grad_input_norm

        def vector_sums(feature_rows, head_rows):
            features = to_absolute(jnp.stack(feature_rows))
            lines = features.shape[0]
            joined = jnp.concatenate([features.reshape(-1, 128)] + [v.reshape(-1, 128) for v in head_rows])
            cut = lines * depth // 128
            for mask in plane + [top]:
                joined = joined + swap(joined, mask)
            tail = joined[cut:]
            sizes = [v.shape[0] // 128 for v in head_rows]
            pieces = []
            offset = 0
            for size in sizes:
                pieces.append(tail[offset : offset + size])
                offset += size
            for mask in middle[::-1]:
                kept = []
                for piece in pieces:
                    size = piece.shape[0] // 2
                    kept.append(piece[:size] + swap(piece[size:], mask))
                pieces = kept
            tail = jnp.concatenate(pieces)
            features = joined[:cut]
            both = jnp.concatenate([features, tail])
            came = swap(both, mate)
            features = features + came[:cut]
            tail = jnp.where(alike, tail, came[cut:])
            for mask in middle + [low]:
                features = features + swap(features, mask)
            outs = []
            offset = 0
            for piece in pieces:
                outs.append(tail[offset : offset + piece.shape[0]].reshape(-1))
                offset += piece.shape[0]
            return features.reshape(lines, depth), outs

        squares_row = jnp.full((depth,), squares, jnp.float32)
        early, (grad_b_up,) = vector_sums(
            [
                grad_gain2,
                grad_shift2,
                jnp.sum(grad_hidden, axis=0),
                jnp.sum(grad_output, axis=0),
                squares_row,
            ],
            [jnp.sum(grad_pre_all.astype(jnp.float32), axis=0)],
        )
        late, (grad_b_query, grad_b_value) = vector_sums(
            [grad_gain1, grad_shift1],
            [
                jnp.sum(grad_pre_query.astype(jnp.float32), axis=0),
                jnp.sum(grad_values.astype(jnp.float32), axis=0),
            ],
        )
        mean_loss = early[4, 0] / (valid_count * depth)
        return (
            to_absolute(narrow(output)),
            mean_loss,
            to_absolute(grad_tokens),
            late[0],
            late[1],
            grad_w_query,
            grad_b_query,
            grad_w_key,
            grad_w_value,
            grad_b_value,
            grad_w_out,
            early[2],
            early[0],
            early[1],
            grad_w_up,
            grad_b_up,
            grad_w_down,
            early[3],
        )

    return body


def solution(mesh):
    placed = (
        P(("fsdp", "tp"), None),
        P(),
        P(),
        P("fsdp", "tp"),
        P("tp"),
        P("fsdp", "tp"),
        P("fsdp", "tp"),
        P("tp"),
        P("fsdp", "tp"),
        P(),
        P(),
        P(),
        P("fsdp", "tp"),
        P("tp"),
        P("fsdp", "tp"),
        P(),
        P(("fsdp", "tp"), None),
        P(("fsdp", "tp")),
        P("fsdp", None),
        P("fsdp", None, None),
    )
    return jax.shard_map(
        make_body(mesh.shape["fsdp"], mesh.shape["tp"]),
        mesh=mesh,
        in_specs=placed,
        out_specs=(
            P(("fsdp", "tp"), None),
            P(),
            P(("fsdp", "tp"), None),
            P(),
            P(),
            P("fsdp", "tp"),
            P("tp"),
            P("fsdp", "tp"),
            P("fsdp", "tp"),
            P("tp"),
            P("fsdp", "tp"),
            P(),
            P(),
            P(),
            P("fsdp", "tp"),
            P("tp"),
            P("fsdp", "tp"),
            P(),
        ),
        check_vma=False,
    )
```

```python
import jax
import jax.numpy as jnp
from jax import lax
from jax.experimental import pallas as pl
from jax.experimental.pallas import tpu as pltpu
from jax.sharding import PartitionSpec as P

HD = 64
PAIR = 2 * HD
EPSILON = 1e-05
MASKED_SCORE = -1e30
KEY_PAD = 128


def layer_norm(vectors, norm_gain, norm_shift):
    centre = jnp.mean(vectors, axis=-1, keepdims=True)
    centred = vectors - centre
    spread = jnp.mean(centred * centred, axis=-1, keepdims=True)
    return centred * lax.rsqrt(spread + EPSILON) * norm_gain + norm_shift


def contract(left_side, right_side, left_dim, right_dim):
    return lax.dot_general(
        left_side,
        right_side,
        (((left_dim,), (right_dim,)), ((), ())),
        preferred_element_type=jnp.float32,
    )


def narrow(values):
    return values.astype(jnp.bfloat16)


def after(values, *needed):
    return lax.optimization_barrier((values, needed))[0]


def bits_below(count, first):
    bits = []
    bit = first
    while bit < count:
        bits.append(bit)
        bit *= 2
    return bits


def segment_scores(q_ref, k_ref, ks_ref, seen_ref, row, seg, tree, place):
    rows = pl.ds(row, seg)
    lane = lax.broadcasted_iota(jnp.int32, (seg, PAIR), 1)
    first_head = lane < HD
    query = q_ref[rows, :]
    none = jnp.zeros_like(query)
    both = jnp.concatenate(
        [jnp.where(first_head, query, none), jnp.where(first_head, none, query)], axis=0
    )
    keys = jnp.concatenate([k_ref[rows, :], ks_ref[tree]], axis=0)
    scores = contract(both, keys, 1, 1)
    width = seg + KEY_PAD
    column = lax.broadcasted_iota(jnp.int32, (2 * seg, width), 1)
    position = lax.broadcasted_iota(jnp.int32, (2 * seg, width), 0)
    position = jnp.where(position >= seg, position - seg, position)
    seen = jnp.concatenate(
        [jnp.ones((1, seg), jnp.float32), seen_ref[pl.ds(place, 1), :]], axis=1
    )
    reach = jnp.where(column < seg, position, width)
    allowed = (column <= reach) & (seen > 0.5)
    scores = jnp.where(allowed, scores, MASKED_SCORE)
    highest = jnp.max(scores, axis=1, keepdims=True)
    raised = jnp.exp(scores - highest)
    probs = raised * (1.0 / jnp.sum(raised, axis=1, keepdims=True))
    return rows, first_head, both, keys, probs


def walk_segments(blocks, rows, seg, step):
    per = rows // seg
    for block in range(blocks):
        tree, far = block % 2, block // 2
        for inner in range(per):
            step(block * rows + inner * seg, tree, (tree * 2 + far) * per + inner)


def forward_kernel(rows, seg, q_ref, k_ref, v_ref, ks_ref, vs_ref, seen_ref, out_ref):
    def step(row, tree, place):
        at, first_head, both, keys, probs = segment_scores(
            q_ref, k_ref, ks_ref, seen_ref, row, seg, tree, place
        )
        values = jnp.concatenate([v_ref[at, :], vs_ref[tree]], axis=0)
        mixed = contract(narrow(probs), values, 1, 0)
        out_ref[at, :] = narrow(jnp.where(first_head, mixed[:seg], mixed[seg:]))

    walk_segments(4, rows, seg, step)


def backward_kernel(
    rows, seg, q_ref, k_ref, v_ref, go_ref, ks_ref, vs_ref, seen_ref, gq_ref, gk_ref, gv_ref, gks_ref, gvs_ref
):
    gks_ref[...] = jnp.zeros_like(gks_ref)
    gvs_ref[...] = jnp.zeros_like(gvs_ref)

    def step(row, tree, place):
        at, first_head, both, keys, probs = segment_scores(
            q_ref, k_ref, ks_ref, seen_ref, row, seg, tree, place
        )
        values = jnp.concatenate([v_ref[at, :], vs_ref[tree]], axis=0)
        grad_out = go_ref[at, :]
        none = jnp.zeros_like(grad_out)
        grad_both = jnp.concatenate(
            [jnp.where(first_head, grad_out, none), jnp.where(first_head, none, grad_out)], axis=0
        )
        grad_probs = contract(grad_both, values, 1, 1)
        inner = jnp.sum(probs * grad_probs, axis=1, keepdims=True)
        grad_scores = narrow(probs * (grad_probs - inner))
        grad_query = contract(grad_scores, keys, 1, 0)
        grad_query = narrow(jnp.where(first_head, grad_query[:seg], grad_query[seg:]))
        gq_ref[at, :] = grad_query * jnp.bfloat16(0.125)
        grad_keys = contract(grad_scores, both, 0, 0)
        gk_ref[at, :] = narrow(grad_keys[:seg])
        gks_ref[tree] += grad_keys[seg:]
        grad_values = contract(narrow(probs), grad_both, 0, 0)
        gv_ref[at, :] = narrow(grad_values[:seg])
        gvs_ref[tree] += grad_values[seg:]

    walk_segments(4, rows, seg, step)


def attend(kernel, rows, seg, operands, key_sums, seen, outputs, sums):
    count, width = operands[0].shape
    column_block = pl.BlockSpec((count, PAIR), lambda pair: (0, pair))
    sum_block = pl.BlockSpec((2, KEY_PAD, PAIR), lambda pair: (0, 0, pair))
    return pl.pallas_call(
        lambda *refs: kernel(rows, seg, *refs),
        grid=(width // PAIR,),
        in_specs=[column_block] * len(operands)
        + [sum_block] * 2
        + [pl.BlockSpec(seen.shape, lambda pair: (0, 0))],
        out_specs=[column_block] * outputs + [sum_block] * sums,
        out_shape=[jax.ShapeDtypeStruct((count, width), jnp.bfloat16)] * outputs
        + [jax.ShapeDtypeStruct((2, KEY_PAD, width), jnp.float32)] * sums,
        cost_estimate=pl.CostEstimate(flops=1, bytes_accessed=1, transcendentals=0),
        name="attend_forward" if sums == 0 else "attend_backward",
    )(*operands, *key_sums, seen)


def make_body(fsdp, tp):
    world = fsdp * tp
    low = 1
    top = tp // 2
    middle = bits_below(top, 2)
    mate = tp
    plane = bits_below(world, 2 * tp)

    def swap(values, mask):
        return lax.ppermute(values, ("fsdp", "tp"), [(i, i ^ mask) for i in range(world)])

    def everyone(values):
        for mask in bits_below(world, tp) + bits_below(tp, 1):
            values = values + swap(values, mask)
        return values

    def body(
        tokens,
        norm1_gain,
        norm1_shift,
        w_query,
        b_query,
        w_key,
        w_value,
        b_value,
        w_out,
        b_out,
        norm2_gain,
        norm2_shift,
        w_up,
        b_up,
        w_down,
        b_down,
        teacher,
        valid_mask,
        parents,
        summary,
    ):
        rows, depth = tokens.shape
        strip = depth // fsdp
        half = depth // 2
        column = lax.axis_index("tp")
        device = lax.axis_index("fsdp")
        core = device % 2
        spot = device // 2
        upper = column // top
        alike = core == upper
        segments = parents.shape[1]
        marks = summary.shape[2]
        seg = rows * tp // segments
        per = rows // seg

        def mirrored(k):
            mirror, found = 0, 0
            for i in range(len(plane)):
                found = (k >> i) & 1
                mirror = mirror * 2 + found
            return mirror

        blocks = fsdp // 2

        def to_relative(values):
            parts = []
            for side in range(2):
                for k in range(blocks):
                    away = k if side == 0 else mirrored(k)
                    start = (2 * (spot ^ away) + side) * strip
                    parts.append(lax.dynamic_slice_in_dim(values, start, strip, values.ndim - 1))
            return jnp.concatenate(parts, axis=-1)

        def to_absolute(values):
            parts = []
            for place in range(blocks):
                away = spot ^ place
                back = jnp.zeros_like(away)
                for i in range(len(plane)):
                    back = back * 2 + ((away >> i) & 1)
                for side in range(2):
                    start = (away if side == 0 else blocks + back) * strip
                    parts.append(lax.dynamic_slice_in_dim(values, start, strip, values.ndim - 1))
            return jnp.concatenate(parts, axis=-1)

        lane = []
        gate = []
        sent = []

        def ship(items):
            values = after([value for value, _ in items], lane[-2:-1], gate)
            sent.append(values)
            got = [swap(value, mask) for value, (_, mask) in zip(values, items)]
            lane.append(got)
            return got

        orders = (plane, plane[::-1])
        slices = tp // 4

        def bring_weight(shard, across):
            mine = jnp.where(alike, shard, across)
            came = swap(jnp.where(alike, across, shard), mate)
            for mask in middle:
                mine = jnp.concatenate([mine, swap(mine, mask)], axis=1)
                came = jnp.concatenate([came, swap(came, mask)], axis=1)
            return [jnp.where(core == side, mine, came) for side in range(2)]

        def run(stages, *needed):
            gate[:] = needed
            next(stages, None)
            gate.clear()

        def finish(stages, *needed):
            gate[:] = needed
            for _ in stages:
                pass
            gate.clear()

        def gather_weight(both, full):
            sides = [[both[0]], [both[1]]]
            for level in range(len(plane)):
                held = [
                    pieces[0] if level == 0 else jnp.concatenate(pieces, axis=0) for pieces in sides
                ]
                got = ship([(held[side], orders[side][level]) for side in range(2)])
                yield
                got = after(got, gate)
                for side in range(2):
                    sides[side].append(got[side])
            full.append(jnp.concatenate(sides[0] + sides[1], axis=0))

        def scatter_weight(pairs, total, *ahead):
            def rows_of(start, stop, needed):
                parts = [
                    contract(after(left, needed)[:, start:stop], right, 0, 0) for left, right in pairs
                ]
                if len(parts) == 1:
                    return parts[0]
                parts = [part.reshape(stop - start, slices, -1) for part in parts]
                return jnp.concatenate(parts, axis=2).reshape(stop - start, -1)

            sums = []
            for level in reversed(range(len(plane))):
                size = half >> (len(plane) - level)
                if sums:
                    away = [narrow(sums[side][size:]) for side in range(2)]
                else:
                    away = [narrow(rows_of(side * half + size, (side + 1) * half, ahead)) for side in range(2)]
                got = ship([(away[side], orders[side][level]) for side in range(2)])
                yield
                got = after(got, gate)
                if sums:
                    sums = [sums[side][:size] + got[side] for side in range(2)]
                else:
                    sums = [rows_of(side * half, side * half + size, away) + got[side] for side in range(2)]
            kept = [narrow(sums[side]) for side in range(2)]
            mine = jnp.where(core == 0, kept[0], kept[1])
            other = jnp.where(core == 0, kept[1], kept[0])
            for mask in middle[::-1]:
                width = mine.shape[1] // 2
                mine = narrow(mine[:, :width].astype(jnp.float32) + swap(mine[:, width:], mask))
                other = narrow(other[:, :width].astype(jnp.float32) + swap(other[:, width:], mask))
            came = swap(other, mate)
            give = jnp.where(alike, came, mine)
            keep = jnp.where(alike, mine, came)
            given.append(give)
            total.append(keep.astype(jnp.float32) + swap(give, top))

        given = []

        def gather_bias(part):
            part = jnp.where(alike, part, swap(part, top))
            for mask in middle:
                part = jnp.concatenate([part, swap(part, mask)], axis=1)
            return part

        def spread_rows(own):
            across = swap(own, low)
            near = jnp.concatenate([own, swap(own, mate)], axis=0)
            far = jnp.concatenate([across, swap(across, mate)], axis=0)
            return near, far

        def start_collect(values, partial):
            far_mate = swap(narrow(partial(row_block(values, 3))), mate)
            leaving = narrow(partial(row_block(values, 2)) + far_mate)
            crossing = swap(leaving, low)
            values = after(values, leaving)
            near_mate = swap(narrow(partial(row_block(values, 1))), mate)
            own = partial(row_block(values, 0))

            def complete(*needed):
                return own + near_mate + after(crossing, needed)

            return leaving, complete

        def row_block(values, block):
            return values[block * rows : (block + 1) * rows]

        inputs = to_relative(tokens).astype(jnp.float32)
        target = to_relative(teacher).astype(jnp.float32)
        vectors = to_relative(
            jnp.stack([norm1_gain, norm1_shift, b_out, norm2_gain, norm2_shift, b_down])
        )
        gain1, shift1, bias_out, gain2, shift2, bias_down = [vectors[i] for i in range(6)]
        weight_mask = valid_mask.astype(jnp.float32)[:, None]
        counted = everyone(jnp.full((8, 128), jnp.sum(weight_mask), jnp.float32))
        valid_count = counted[0, 0]

        shards = [
            jnp.concatenate([w_key, w_value], axis=1),
            jnp.concatenate([w_query, w_out], axis=1),
            w_up,
            w_down,
        ]
        crossed = []

        gathered = [[], [], [], []]

        leaving_shards = []

        def cross(which, *needed):
            leaving_shards.append(after(shards[which], needed))
            crossed.append(swap(leaving_shards[-1], top))

        def fetch(which, *needed):
            across = after(crossed[which], needed)
            return gather_weight(bring_weight(shards[which], across), gathered[which])

        cross(0)
        kv_stages = fetch(0)
        run(kv_stages)
        cross(1, crossed[0])
        run(kv_stages)
        cross(2, lane[0])
        qo_stages = fetch(1, sent[-1])
        run(qo_stages)
        finish(kv_stages)
        finish(qo_stages)
        up_stages = fetch(2, lane[-1])
        run(up_stages)
        w_kv, w_qo = gathered[0][0], gathered[1][0]

        def split_two(joined):
            parts = joined.reshape(joined.shape[0], slices, 2, -1)
            return [parts[:, :, i].reshape(joined.shape[0], -1) for i in range(2)]

        full_key, full_value = split_two(w_kv)
        full_query, full_out = split_two(w_qo)
        bias = gather_bias(jnp.concatenate([b_query, b_value, b_up])[None]).reshape(slices, -1)
        heads = b_query.shape[0]
        bias_query = bias[:, :heads].reshape(-1)
        bias_value = bias[:, heads : 2 * heads].reshape(-1)
        bias_up = bias[:, 2 * heads :].reshape(-1)

        tables = jnp.concatenate([parents[0][:, None], summary[0]], axis=1)
        tables = jnp.stack([tables, swap(tables, mate)])
        seg_ids = jnp.arange(segments, dtype=jnp.int32)
        moved = seg_ids ^ (column * per)
        picks = moved[:, None] == seg_ids[None, :]
        tables = jnp.sum(jnp.where(picks[None, :, :, None], tables[:, None], 0), axis=2)
        parent_rel = jnp.where(tables[:, :, 0] >= 0, tables[:, :, 0] ^ (column * per), -1)
        offsets_rel = tables[:, :, 1:]
        reach = (parent_rel[:, :, None] == seg_ids[None, None, :]).astype(jnp.float32)
        unit = (seg_ids[:, None] == seg_ids[None, :]).astype(jnp.float32)[None]
        closure = reach + unit
        steps = 1
        while steps < segments:
            closure = jnp.einsum("tij,tjk->tik", closure, closure)
            closure = jnp.minimum(closure, 1.0)
            steps *= 2
        closure = closure - unit
        local = 2 * per
        seen = jnp.repeat(closure[:, :local], marks, axis=2)
        seen = jnp.pad(seen, ((0, 0), (0, 0), (0, KEY_PAD - segments * marks)))
        seen = seen.reshape(2 * local, KEY_PAD)
        far_id = jnp.arange(local, dtype=jnp.int32) // per
        inner_id = jnp.arange(local, dtype=jnp.int32) % per
        tree_id = jnp.arange(2, dtype=jnp.int32)
        start = (far_id[None, :] * 2 + tree_id[:, None]) * rows + inner_id[None, :] * seg
        summary_row = (start[:, :, None] + offsets_rel[:, :local]).reshape(-1)
        chosen = narrow(summary_row[:, None] == jnp.arange(4 * rows, dtype=jnp.int32)[None, :])

        def spread_sums(part, needed):
            for mask in middle + [top]:
                part = jnp.concatenate([part, after(swap(part, mask), needed)], axis=1)
            return jnp.pad(part, ((0, 0), (0, KEY_PAD - part.shape[1]), (0, 0)))

        def collect_sums(whole):
            whole = whole[:, : segments * marks]
            for mask in [top] + middle[::-1]:
                size = whole.shape[1] // 2
                whole = whole[:, :size] + swap(narrow(whole[:, size:]), mask)
            return whole

        normed = narrow(layer_norm(inputs, gain1, shift1))
        normed_near, normed_far = spread_rows(after(normed, crossed[0], valid_count, bias, tables))
        normed_all = jnp.concatenate([normed_near, normed_far], axis=0)
        key_states = narrow(contract(normed_all, full_key, 1, 0))
        value_states = narrow(contract(normed_all, full_value, 1, 0) + bias_value)
        queries = narrow((contract(normed_all, full_query, 1, 0) + bias_query) * 0.125)
        width = queries.shape[1]
        picked = jnp.concatenate(
            [narrow(contract(chosen, key_states, 1, 0)), narrow(contract(chosen, value_states, 1, 0))],
            axis=1,
        )
        picked = picked.reshape(2, local * marks, 2 * width)
        cross(3, crossed[2], picked)
        queries = after(queries, leaving_shards[-1], sent[-1])
        picked = spread_sums(picked, queries)
        key_sums = (picked[:, :, :width], picked[:, :, width:])
        (attended,) = attend(
            forward_kernel, rows, seg, (queries, key_states, value_states), key_sums, seen, 1, 0
        )
        leaving, complete = start_collect(attended, lambda block: contract(block, full_out, 1, 1))
        run(up_stages, leaving)
        branch = complete(sent[-1])
        hidden = inputs + branch + bias_out

        normed_mid = narrow(layer_norm(hidden, gain2, shift2))
        down_stages = fetch(3, normed_mid)
        run(down_stages)
        finish(up_stages, normed_mid)
        mid_near, mid_far = spread_rows(normed_mid)
        mid_far = after(mid_far, sent[-1])
        full_up = gathered[2][0]
        active = []
        for part in (mid_near, mid_far):
            part = after(part, active)
            active.append(narrow(jnp.maximum(contract(part, full_up, 1, 0) + bias_up, 0.0)))
        run(down_stages, active)
        finish(down_stages)
        full_down = gathered[3][0]
        active_all = jnp.concatenate(active, axis=0)
        mid_all = jnp.concatenate([mid_near, mid_far], axis=0)
        _, complete = start_collect(active_all, lambda block: contract(block, full_down, 1, 1))
        feed_out = complete()
        output = hidden + feed_out + bias_down

        deviation = output - target
        squares = jnp.sum(weight_mask * deviation * deviation)
        total_tokens = rows * world
        grad_output = (2.0 * total_tokens / valid_count) * weight_mask * deviation

        feed_near, feed_far = spread_rows(narrow(grad_output))
        feed_all = jnp.concatenate([feed_near, feed_far], axis=0)
        totals = [[], [], [], []]
        down_stages = scatter_weight([(feed_all, active_all)], totals[0])
        run(down_stages)
        feed_near, feed_far = after((feed_near, feed_far), sent[-1])
        grad_pre = []
        for part, kept in zip((feed_near, feed_far), active):
            part = after(part, grad_pre)
            grad_pre.append(narrow(jnp.where(kept > 0, contract(part, full_down, 1, 0), 0.0)))
        grad_pre_all = jnp.concatenate(grad_pre, axis=0)
        mid_leaving, complete = start_collect(grad_pre_all, lambda block: contract(block, full_up, 1, 1))
        up_stages = scatter_weight([(mid_all, grad_pre_all)], totals[1], mid_leaving)
        run(up_stages)
        run(down_stages, sent[-1])
        grad_mid = complete(sent[-1])
        second_norm, second_pull = jax.vjp(layer_norm, hidden, gain2, shift2)
        grad_hidden_norm, grad_gain2, grad_shift2 = second_pull(grad_mid)
        grad_hidden = grad_output + grad_hidden_norm

        grad_branch = narrow(grad_hidden)
        branch_near, branch_far = spread_rows(grad_branch)
        run(up_stages, grad_branch)
        branch_far = after(branch_far, sent[-1])
        branch_all = jnp.concatenate([branch_near, branch_far], axis=0)
        grad_attended = narrow(contract(branch_all, full_out, 1, 0))
        grad_pre_query, grad_keys, grad_values, key_part, value_part = attend(
            backward_kernel,
            rows,
            seg,
            (queries, key_states, value_states, grad_attended),
            key_sums,
            seen,
            3,
            2,
        )
        parts = collect_sums(jnp.concatenate([key_part, value_part], axis=2))
        parts = narrow(parts.reshape(-1, 2 * width))
        grad_keys = narrow(grad_keys + contract(chosen, parts[:, :width], 0, 0))
        grad_values = narrow(grad_values + contract(chosen, parts[:, width:], 0, 0))
        joined_grads = jnp.concatenate([grad_keys, grad_values, grad_pre_query], axis=1)

        def normed_part(block):
            return (
                contract(block[:, :width], full_key, 1, 1)
                + contract(block[:, width : 2 * width], full_value, 1, 1)
                + contract(block[:, 2 * width :], full_query, 1, 1)
            )

        normed_leaving, complete = start_collect(joined_grads, normed_part)
        first_stages = scatter_weight(
            [(branch_all, attended), (normed_all, grad_pre_query)], totals[2], normed_leaving
        )
        run(first_stages, normed_leaving)
        last_stages = scatter_weight(
            [(normed_all, grad_keys), (normed_all, grad_values)], totals[3], sent[-1]
        )
        finish(down_stages, normed_leaving)
        run(last_stages, given[0])
        finish(up_stages, given[0])
        grad_normed = complete(sent[-1])
        first_norm, first_pull = jax.vjp(layer_norm, inputs, gain1, shift1)
        grad_input_norm, grad_gain1, grad_shift1 = first_pull(grad_normed)
        grad_tokens = grad_hidden + grad_input_norm

        feature_rows = [
            grad_gain2,
            grad_shift2,
            jnp.sum(grad_hidden, axis=0),
            jnp.sum(grad_output, axis=0),
            jnp.full((depth,), squares, jnp.float32),
            grad_gain1,
            grad_shift1,
        ]
        head_rows = [
            jnp.sum(grad_pre_all.astype(jnp.float32), axis=0),
            jnp.sum(grad_pre_query.astype(jnp.float32), axis=0),
            jnp.sum(grad_values.astype(jnp.float32), axis=0),
        ]
        lines = len(feature_rows)
        cut = lines * depth // 128
        joined = to_absolute(jnp.stack(feature_rows)).reshape(-1, 128)
        joined = jnp.concatenate([joined] + [v.reshape(-1, 128) for v in head_rows])
        turns = [first_stages, last_stages]
        for turn, mask in enumerate(plane):
            came = swap(joined, mask)
            run(turns[turn % 2], given[1])
            joined = joined + after(came, sent[-1])
        came = swap(joined, mate)
        finish(first_stages)
        came = after(came, given[2])
        features = joined[:cut] + came[:cut]
        tails = [jnp.where(alike, joined[cut:], came[cut:]), jnp.where(alike, came[cut:], joined[cut:])]
        sizes = [v.shape[0] // 128 for v in head_rows]
        for mask in middle[::-1]:
            for which, tail in enumerate(tails):
                keep, give, offset = [], [], 0
                for size in sizes:
                    keep.append(tail[offset : offset + size // 2])
                    give.append(tail[offset + size // 2 : offset + size])
                    offset += size
                tails[which] = jnp.concatenate(keep) + swap(jnp.concatenate(give), mask)
            sizes = [size // 2 for size in sizes]
        for mask in middle + [low]:
            came = swap(features, mask)
            finish(last_stages)
            features = features + after(came, given[3])
        came = swap(jnp.concatenate([features, tails[1]]), top)
        features = (features + came[:cut]).reshape(lines, depth)
        tail = tails[0] + came[cut:]
        ends = [sum(sizes[: i + 1]) for i in range(len(sizes))]
        grad_b_up, grad_b_query, grad_b_value = [
            tail[end - size : end].reshape(-1) for end, size in zip(ends, sizes)
        ]
        grad_w_down, grad_w_up = totals[0][0], totals[1][0]
        grad_w_out, grad_w_query = jnp.split(totals[2][0], 2, axis=1)
        grad_w_key, grad_w_value = jnp.split(totals[3][0], 2, axis=1)
        mean_loss = features[4, 0] / (valid_count * depth)
        return (
            to_absolute(narrow(output)),
            mean_loss,
            to_absolute(grad_tokens),
            features[5],
            features[6],
            grad_w_query,
            grad_b_query,
            grad_w_key,
            grad_w_value,
            grad_b_value,
            grad_w_out,
            features[2],
            features[0],
            features[1],
            grad_w_up,
            grad_b_up,
            grad_w_down,
            features[3],
        )

    return body


def solution(mesh):
    placed = (
        P(("fsdp", "tp"), None),
        P(),
        P(),
        P("fsdp", "tp"),
        P("tp"),
        P("fsdp", "tp"),
        P("fsdp", "tp"),
        P("tp"),
        P("fsdp", "tp"),
        P(),
        P(),
        P(),
        P("fsdp", "tp"),
        P("tp"),
        P("fsdp", "tp"),
        P(),
        P(("fsdp", "tp"), None),
        P(("fsdp", "tp")),
        P("fsdp", None),
        P("fsdp", None, None),
    )
    return jax.shard_map(
        make_body(mesh.shape["fsdp"], mesh.shape["tp"]),
        mesh=mesh,
        in_specs=placed,
        out_specs=(
            P(("fsdp", "tp"), None),
            P(),
            P(("fsdp", "tp"), None),
            P(),
            P(),
            P("fsdp", "tp"),
            P("tp"),
            P("fsdp", "tp"),
            P("fsdp", "tp"),
            P("tp"),
            P("fsdp", "tp"),
            P(),
            P(),
            P(),
            P("fsdp", "tp"),
            P("tp"),
            P("fsdp", "tp"),
            P(),
        ),
        check_vma=False,
    )
```

```python
import jax
import jax.numpy as jnp
from jax import lax
from jax.experimental import pallas as pl
from jax.experimental.pallas import tpu as pltpu
from jax.sharding import PartitionSpec as P

HD = 64
PAIR = 2 * HD
EPSILON = 1e-05
MASKED_SCORE = -1e30
KEY_PAD = 128


def layer_norm(vectors, norm_gain, norm_shift):
    centre = jnp.mean(vectors, axis=-1, keepdims=True)
    centred = vectors - centre
    spread = jnp.mean(centred * centred, axis=-1, keepdims=True)
    return centred * lax.rsqrt(spread + EPSILON) * norm_gain + norm_shift


def contract(left_side, right_side, left_dim, right_dim):
    return lax.dot_general(
        left_side,
        right_side,
        (((left_dim,), (right_dim,)), ((), ())),
        preferred_element_type=jnp.float32,
    )


def narrow(values):
    return values.astype(jnp.bfloat16)


def after(values, *needed):
    return lax.optimization_barrier((values, needed))[0]


def bits_below(count, first):
    bits = []
    bit = first
    while bit < count:
        bits.append(bit)
        bit *= 2
    return bits


def segment_scores(q_ref, k_ref, ks_ref, seen_ref, row, seg, tree, place):
    rows = pl.ds(row, seg)
    lane = lax.broadcasted_iota(jnp.int32, (seg, PAIR), 1)
    first_head = lane < HD
    query = q_ref[rows, :]
    none = jnp.zeros_like(query)
    both = jnp.concatenate(
        [jnp.where(first_head, query, none), jnp.where(first_head, none, query)], axis=0
    )
    keys = jnp.concatenate([k_ref[rows, :], ks_ref[tree]], axis=0)
    scores = contract(both, keys, 1, 1)
    width = seg + KEY_PAD
    column = lax.broadcasted_iota(jnp.int32, (2 * seg, width), 1)
    position = lax.broadcasted_iota(jnp.int32, (2 * seg, width), 0)
    position = jnp.where(position >= seg, position - seg, position)
    seen = jnp.concatenate(
        [jnp.ones((1, seg), jnp.float32), seen_ref[pl.ds(place, 1), :]], axis=1
    )
    reach = jnp.where(column < seg, position, width)
    allowed = (column <= reach) & (seen > 0.5)
    scores = jnp.where(allowed, scores, MASKED_SCORE)
    highest = jnp.max(scores, axis=1, keepdims=True)
    raised = jnp.exp(scores - highest)
    probs = raised * (1.0 / jnp.sum(raised, axis=1, keepdims=True))
    return rows, first_head, both, keys, probs


def walk_segments(blocks, rows, seg, step):
    per = rows // seg
    for block in range(blocks):
        tree, far = block % 2, block // 2
        for inner in range(per):
            step(block * rows + inner * seg, tree, (tree * 2 + far) * per + inner)


def forward_kernel(rows, seg, q_ref, k_ref, v_ref, ks_ref, vs_ref, seen_ref, out_ref):
    def step(row, tree, place):
        at, first_head, both, keys, probs = segment_scores(
            q_ref, k_ref, ks_ref, seen_ref, row, seg, tree, place
        )
        values = jnp.concatenate([v_ref[at, :], vs_ref[tree]], axis=0)
        mixed = contract(narrow(probs), values, 1, 0)
        out_ref[at, :] = narrow(jnp.where(first_head, mixed[:seg], mixed[seg:]))

    walk_segments(4, rows, seg, step)


def backward_kernel(
    rows, seg, q_ref, k_ref, v_ref, go_ref, ks_ref, vs_ref, seen_ref, gq_ref, gk_ref, gv_ref, gks_ref, gvs_ref
):
    gks_ref[...] = jnp.zeros_like(gks_ref)
    gvs_ref[...] = jnp.zeros_like(gvs_ref)

    def step(row, tree, place):
        at, first_head, both, keys, probs = segment_scores(
            q_ref, k_ref, ks_ref, seen_ref, row, seg, tree, place
        )
        values = jnp.concatenate([v_ref[at, :], vs_ref[tree]], axis=0)
        grad_out = go_ref[at, :]
        none = jnp.zeros_like(grad_out)
        grad_both = jnp.concatenate(
            [jnp.where(first_head, grad_out, none), jnp.where(first_head, none, grad_out)], axis=0
        )
        grad_probs = contract(grad_both, values, 1, 1)
        inner = jnp.sum(probs * grad_probs, axis=1, keepdims=True)
        grad_scores = narrow(probs * (grad_probs - inner))
        grad_query = contract(grad_scores, keys, 1, 0)
        grad_query = narrow(jnp.where(first_head, grad_query[:seg], grad_query[seg:]))
        gq_ref[at, :] = grad_query * jnp.bfloat16(0.125)
        grad_keys = contract(grad_scores, both, 0, 0)
        gk_ref[at, :] = narrow(grad_keys[:seg])
        gks_ref[tree] += grad_keys[seg:]
        grad_values = contract(narrow(probs), grad_both, 0, 0)
        gv_ref[at, :] = narrow(grad_values[:seg])
        gvs_ref[tree] += grad_values[seg:]

    walk_segments(4, rows, seg, step)


def attend(kernel, rows, seg, operands, key_sums, seen, outputs, sums):
    count, width = operands[0].shape
    column_block = pl.BlockSpec((count, PAIR), lambda pair: (0, pair))
    sum_block = pl.BlockSpec((2, KEY_PAD, PAIR), lambda pair: (0, 0, pair))
    return pl.pallas_call(
        lambda *refs: kernel(rows, seg, *refs),
        grid=(width // PAIR,),
        in_specs=[column_block] * len(operands)
        + [sum_block] * 2
        + [pl.BlockSpec(seen.shape, lambda pair: (0, 0))],
        out_specs=[column_block] * outputs + [sum_block] * sums,
        out_shape=[jax.ShapeDtypeStruct((count, width), jnp.bfloat16)] * outputs
        + [jax.ShapeDtypeStruct((2, KEY_PAD, width), jnp.float32)] * sums,
        cost_estimate=pl.CostEstimate(flops=1, bytes_accessed=1, transcendentals=0),
        name="attend_forward" if sums == 0 else "attend_backward",
    )(*operands, *key_sums, seen)


def make_body(fsdp, tp):
    world = fsdp * tp
    low = 1
    top = tp // 2
    middle = bits_below(top, 2)
    mate = tp
    plane = bits_below(world, 2 * tp)

    def swap(values, mask):
        return lax.ppermute(values, ("fsdp", "tp"), [(i, i ^ mask) for i in range(world)])

    def body(
        tokens,
        norm1_gain,
        norm1_shift,
        w_query,
        b_query,
        w_key,
        w_value,
        b_value,
        w_out,
        b_out,
        norm2_gain,
        norm2_shift,
        w_up,
        b_up,
        w_down,
        b_down,
        teacher,
        valid_mask,
        parents,
        summary,
    ):
        rows, depth = tokens.shape
        strip = depth // fsdp
        half = depth // 2
        column = lax.axis_index("tp")
        device = lax.axis_index("fsdp")
        core = device % 2
        spot = device // 2
        upper = column // top
        alike = core == upper
        segments = parents.shape[1]
        marks = summary.shape[2]
        seg = rows * tp // segments
        per = rows // seg

        def mirrored(k):
            mirror, found = 0, 0
            for i in range(len(plane)):
                found = (k >> i) & 1
                mirror = mirror * 2 + found
            return mirror

        blocks = fsdp // 2

        def to_relative(values):
            parts = []
            for side in range(2):
                for k in range(blocks):
                    away = k if side == 0 else mirrored(k)
                    start = (2 * (spot ^ away) + side) * strip
                    parts.append(lax.dynamic_slice_in_dim(values, start, strip, values.ndim - 1))
            return jnp.concatenate(parts, axis=-1)

        def to_absolute(values):
            parts = []
            for place in range(blocks):
                away = spot ^ place
                back = jnp.zeros_like(away)
                for i in range(len(plane)):
                    back = back * 2 + ((away >> i) & 1)
                for side in range(2):
                    start = (away if side == 0 else blocks + back) * strip
                    parts.append(lax.dynamic_slice_in_dim(values, start, strip, values.ndim - 1))
            return jnp.concatenate(parts, axis=-1)

        lane = []
        gate = []
        sent = []

        def ship(items):
            values = after([value for value, _ in items], lane[-2:-1], gate)
            sent.append(values)
            got = [swap(value, mask) for value, (_, mask) in zip(values, items)]
            lane.append(got)
            return got

        orders = (plane, plane[::-1])
        slices = tp // 4

        def bring_weight(shard, across):
            mine = jnp.where(alike, shard, across)
            came = swap(jnp.where(alike, across, shard), mate)
            for mask in middle:
                mine = jnp.concatenate([mine, swap(mine, mask)], axis=1)
                came = jnp.concatenate([came, swap(came, mask)], axis=1)
            return [jnp.where(core == side, mine, came) for side in range(2)]

        def run(stages, *needed):
            gate[:] = needed
            next(stages, None)
            gate.clear()

        def finish(stages, *needed):
            gate[:] = needed
            for _ in stages:
                pass
            gate.clear()

        def gather_weight(both, full):
            sides = [[both[0]], [both[1]]]
            for level in range(len(plane)):
                held = [
                    pieces[0] if level == 0 else jnp.concatenate(pieces, axis=0) for pieces in sides
                ]
                got = ship([(held[side], orders[side][level]) for side in range(2)])
                yield
                got = after(got, gate)
                for side in range(2):
                    sides[side].append(got[side])
            full.append(jnp.concatenate(sides[0] + sides[1], axis=0))

        def scatter_weight(pairs, total, *ahead):
            def rows_of(start, stop, needed):
                parts = [
                    contract(after(left, needed)[:, start:stop], right, 0, 0) for left, right in pairs
                ]
                if len(parts) == 1:
                    return parts[0]
                parts = [part.reshape(stop - start, slices, -1) for part in parts]
                return jnp.concatenate(parts, axis=2).reshape(stop - start, -1)

            sums = []
            for level in reversed(range(len(plane))):
                size = half >> (len(plane) - level)
                if sums:
                    away = [narrow(sums[side][size:]) for side in range(2)]
                else:
                    away = [narrow(rows_of(side * half + size, (side + 1) * half, ahead)) for side in range(2)]
                got = ship([(away[side], orders[side][level]) for side in range(2)])
                yield
                got = after(got, gate)
                if sums:
                    sums = [sums[side][:size] + got[side] for side in range(2)]
                else:
                    sums = [rows_of(side * half, side * half + size, away) + got[side] for side in range(2)]
            kept = [narrow(sums[side]) for side in range(2)]
            mine = jnp.where(core == 0, kept[0], kept[1])
            other = jnp.where(core == 0, kept[1], kept[0])
            for mask in middle[::-1]:
                width = mine.shape[1] // 2
                mine = narrow(mine[:, :width].astype(jnp.float32) + swap(mine[:, width:], mask))
                other = narrow(other[:, :width].astype(jnp.float32) + swap(other[:, width:], mask))
            came = swap(other, mate)
            give = jnp.where(alike, came, mine)
            keep = jnp.where(alike, mine, came)
            given.append(give)
            total.append(keep.astype(jnp.float32) + swap(give, top))

        given = []

        def gather_bias(part):
            part = jnp.where(alike, part, swap(part, top))
            for mask in middle:
                part = jnp.concatenate([part, swap(part, mask)], axis=1)
            return part

        def spread_rows(own, *needed):
            across = after(swap(own, low), needed)
            near = jnp.concatenate([own, swap(own, mate)], axis=0)
            far = jnp.concatenate([across, swap(across, mate)], axis=0)
            return near, far

        def start_collect(values, partial):
            far_mate = swap(narrow(partial(row_block(values, 3))), mate)
            leaving = narrow(partial(row_block(values, 2)) + far_mate)
            crossing = swap(leaving, low)
            values = after(values, leaving)
            near_mate = swap(narrow(partial(row_block(values, 1))), mate)
            own = partial(row_block(values, 0))

            def complete(*needed):
                return own + near_mate + after(crossing, needed)

            return leaving, complete

        def row_block(values, block):
            return values[block * rows : (block + 1) * rows]

        inputs = to_relative(tokens).astype(jnp.float32)
        target = to_relative(teacher).astype(jnp.float32)
        vectors = to_relative(
            jnp.stack([norm1_gain, norm1_shift, b_out, norm2_gain, norm2_shift, b_down])
        )
        gain1, shift1, bias_out, gain2, shift2, bias_down = [vectors[i] for i in range(6)]
        weight_mask = valid_mask.astype(jnp.float32)[:, None]
        counted = jnp.full((8, 128), jnp.sum(weight_mask), jnp.float32)
        for mask in bits_below(world, tp):
            counted = counted + swap(counted, mask)
        counted = counted + sum(swap(counted, mask) for mask in range(1, tp))
        valid_count = counted[0, 0]

        shards = [
            jnp.concatenate([w_key, w_value], axis=1),
            jnp.concatenate([w_query, w_out], axis=1),
            w_up,
            w_down,
        ]
        crossed = []

        gathered = [[], [], [], []]

        leaving_shards = []

        def cross(which, *needed):
            leaving_shards.append(after(shards[which], needed))
            crossed.append(swap(leaving_shards[-1], top))

        def fetch(which, *needed):
            across = after(crossed[which], needed)
            return gather_weight(bring_weight(shards[which], across), gathered[which])

        cross(0)
        kv_stages = fetch(0, counted)
        run(kv_stages)
        cross(1, crossed[0])
        run(kv_stages)
        cross(2, lane[0])
        qo_stages = fetch(1, sent[-1])
        run(qo_stages)
        finish(kv_stages)
        run(qo_stages, crossed[2])
        up_stages = fetch(2, sent[-1])
        run(up_stages)
        cross(3, crossed[2])
        finish(qo_stages)
        w_kv, w_qo = gathered[0][0], gathered[1][0]

        def split_two(joined):
            parts = joined.reshape(joined.shape[0], slices, 2, -1)
            return [parts[:, :, i].reshape(joined.shape[0], -1) for i in range(2)]

        full_key, full_value = split_two(w_kv)
        full_query, full_out = split_two(w_qo)
        bias = gather_bias(jnp.concatenate([b_query, b_value, b_up])[None]).reshape(slices, -1)
        heads = b_query.shape[0]
        bias_query = bias[:, :heads].reshape(-1)
        bias_value = bias[:, heads : 2 * heads].reshape(-1)
        bias_up = bias[:, 2 * heads :].reshape(-1)

        tables = jnp.concatenate([parents[0][:, None], summary[0]], axis=1)
        tables = jnp.stack([tables, swap(tables, mate)])
        seg_ids = jnp.arange(segments, dtype=jnp.int32)
        moved = seg_ids ^ (column * per)
        picks = moved[:, None] == seg_ids[None, :]
        tables = jnp.sum(jnp.where(picks[None, :, :, None], tables[:, None], 0), axis=2)
        parent_rel = jnp.where(tables[:, :, 0] >= 0, tables[:, :, 0] ^ (column * per), -1)
        offsets_rel = tables[:, :, 1:]
        reach = (parent_rel[:, :, None] == seg_ids[None, None, :]).astype(jnp.float32)
        unit = (seg_ids[:, None] == seg_ids[None, :]).astype(jnp.float32)[None]
        closure = reach + unit
        steps = 1
        while steps < segments:
            closure = jnp.einsum("tij,tjk->tik", closure, closure)
            closure = jnp.minimum(closure, 1.0)
            steps *= 2
        closure = closure - unit
        local = 2 * per
        seen = jnp.repeat(closure[:, :local], marks, axis=2)
        seen = jnp.pad(seen, ((0, 0), (0, 0), (0, KEY_PAD - segments * marks)))
        seen = seen.reshape(2 * local, KEY_PAD)
        far_id = jnp.arange(local, dtype=jnp.int32) // per
        inner_id = jnp.arange(local, dtype=jnp.int32) % per
        tree_id = jnp.arange(2, dtype=jnp.int32)
        start = (far_id[None, :] * 2 + tree_id[:, None]) * rows + inner_id[None, :] * seg
        summary_row = (start[:, :, None] + offsets_rel[:, :local]).reshape(-1)
        chosen = narrow(summary_row[:, None] == jnp.arange(4 * rows, dtype=jnp.int32)[None, :])

        def spread_sums(part, needed):
            for mask in middle + [top]:
                part = jnp.concatenate([part, after(swap(part, mask), needed)], axis=1)
            return jnp.pad(part, ((0, 0), (0, KEY_PAD - part.shape[1]), (0, 0)))

        def collect_sums(whole, *needed):
            whole = whole[:, : segments * marks]
            for mask in [top] + middle[::-1]:
                size = whole.shape[1] // 2
                whole = whole[:, :size] + after(swap(narrow(whole[:, size:]), mask), needed)
            return whole

        normed = narrow(layer_norm(inputs, gain1, shift1))
        normed_near, normed_far = spread_rows(after(normed, crossed[0], bias, tables))
        normed_all = jnp.concatenate([normed_near, normed_far], axis=0)
        key_states = narrow(contract(normed_all, full_key, 1, 0))
        value_states = narrow(contract(normed_all, full_value, 1, 0) + bias_value)
        queries = narrow((contract(normed_all, full_query, 1, 0) + bias_query) * 0.125)
        width = queries.shape[1]
        picked = jnp.concatenate(
            [narrow(contract(chosen, key_states, 1, 0)), narrow(contract(chosen, value_states, 1, 0))],
            axis=1,
        )
        picked = picked.reshape(2, local * marks, 2 * width)
        queries = after(queries, lane[-1], crossed[3])
        picked = spread_sums(picked, queries)
        key_sums = (picked[:, :, :width], picked[:, :, width:])
        (attended,) = attend(
            forward_kernel, rows, seg, (queries, key_states, value_states), key_sums, seen, 1, 0
        )
        leaving, complete = start_collect(attended, lambda block: contract(block, full_out, 1, 1))
        run(up_stages, leaving)
        branch = complete(sent[-1])
        hidden = inputs + branch + bias_out

        normed_mid = narrow(layer_norm(hidden, gain2, shift2))
        down_stages = fetch(3, normed_mid)
        run(down_stages)
        finish(up_stages, normed_mid)
        mid_near, mid_far = spread_rows(normed_mid, lane[-1])
        run(down_stages)
        mid_far = after(mid_far, sent[-1])
        full_up = gathered[2][0]
        active = []
        for part in (mid_near, mid_far):
            part = after(part, active)
            active.append(narrow(jnp.maximum(contract(part, full_up, 1, 0) + bias_up, 0.0)))
        finish(down_stages)
        full_down = gathered[3][0]
        active_all = jnp.concatenate(active, axis=0)
        mid_all = jnp.concatenate([mid_near, mid_far], axis=0)
        _, complete = start_collect(active_all, lambda block: contract(block, full_down, 1, 1))
        feed_out = complete()
        output = hidden + feed_out + bias_down

        deviation = output - target
        squares = jnp.sum(weight_mask * deviation * deviation)
        total_tokens = rows * world
        grad_output = (2.0 * total_tokens / valid_count) * weight_mask * deviation

        feed_near, feed_far = spread_rows(narrow(grad_output))
        feed_all = jnp.concatenate([feed_near, feed_far], axis=0)
        totals = [[], [], [], []]
        down_stages = scatter_weight([(feed_all, active_all)], totals[0])
        run(down_stages)
        feed_near, feed_far = after((feed_near, feed_far), sent[-1])
        grad_pre = []
        for part, kept in zip((feed_near, feed_far), active):
            part = after(part, grad_pre)
            grad_pre.append(narrow(jnp.where(kept > 0, contract(part, full_down, 1, 0), 0.0)))
        grad_pre_all = jnp.concatenate(grad_pre, axis=0)
        mid_leaving, complete = start_collect(grad_pre_all, lambda block: contract(block, full_up, 1, 1))
        up_stages = scatter_weight([(mid_all, grad_pre_all)], totals[1], mid_leaving)
        run(up_stages)
        run(down_stages, sent[-1])
        grad_mid = complete(sent[-1])
        second_norm, second_pull = jax.vjp(layer_norm, hidden, gain2, shift2)
        grad_hidden_norm, grad_gain2, grad_shift2 = second_pull(grad_mid)
        grad_hidden = grad_output + grad_hidden_norm

        grad_branch = narrow(grad_hidden)
        branch_near, branch_far = spread_rows(grad_branch)
        run(up_stages, grad_branch)
        finish(down_stages, sent[-1])
        branch_far = after(branch_far, given[0])
        branch_all = jnp.concatenate([branch_near, branch_far], axis=0)
        grad_attended = narrow(contract(branch_all, full_out, 1, 0))
        grad_pre_query, grad_keys, grad_values, key_part, value_part = attend(
            backward_kernel,
            rows,
            seg,
            (queries, key_states, value_states, grad_attended),
            key_sums,
            seen,
            3,
            2,
        )
        first_stages = scatter_weight(
            [(branch_all, attended), (normed_all, grad_pre_query)], totals[2], grad_pre_query
        )
        run(first_stages)
        finish(up_stages, sent[-1])
        key_part, value_part = after((key_part, value_part), sent[-1])
        parts = collect_sums(jnp.concatenate([key_part, value_part], axis=2), given[1], totals[0])
        parts = narrow(parts.reshape(-1, 2 * width))
        grad_keys = narrow(grad_keys + contract(chosen, parts[:, :width], 0, 0))
        grad_values = narrow(grad_values + contract(chosen, parts[:, width:], 0, 0))
        joined_grads = jnp.concatenate([grad_keys, grad_values, grad_pre_query], axis=1)

        def normed_part(block):
            return (
                contract(block[:, :width], full_key, 1, 1)
                + contract(block[:, width : 2 * width], full_value, 1, 1)
                + contract(block[:, 2 * width :], full_query, 1, 1)
            )

        normed_leaving, complete = start_collect(joined_grads, normed_part)
        last_stages = scatter_weight(
            [(normed_all, grad_keys), (normed_all, grad_values)], totals[3], normed_leaving
        )
        run(last_stages)
        late = sent[-1]
        grad_normed = complete(late)
        run(first_stages, given[1])
        run(last_stages, totals[1])
        finish(first_stages, late)
        finish(last_stages)
        first_norm, first_pull = jax.vjp(layer_norm, inputs, gain1, shift1)
        grad_input_norm, grad_gain1, grad_shift1 = first_pull(grad_normed)
        grad_tokens = grad_hidden + grad_input_norm

        feature_rows = [
            grad_gain2,
            grad_shift2,
            jnp.sum(grad_hidden, axis=0),
            jnp.sum(grad_output, axis=0),
            jnp.full((depth,), squares, jnp.float32),
            grad_gain1,
            grad_shift1,
        ]
        head_rows = [
            jnp.sum(grad_pre_all.astype(jnp.float32), axis=0),
            jnp.sum(grad_pre_query.astype(jnp.float32), axis=0),
            jnp.sum(grad_values.astype(jnp.float32), axis=0),
        ]
        lines = len(feature_rows)
        cut = lines * depth // 128
        joined = to_absolute(jnp.stack(feature_rows)).reshape(-1, 128)
        joined = jnp.concatenate([joined] + [v.reshape(-1, 128) for v in head_rows])
        for mask in plane:
            joined = joined + after(swap(joined, mask), lane[-1] if mask == plane[-1] else sent[-1])
        came = swap(joined, mate)
        features = joined[:cut] + came[:cut]
        tails = [jnp.where(alike, joined[cut:], came[cut:]), jnp.where(alike, came[cut:], joined[cut:])]
        sizes = [v.shape[0] // 128 for v in head_rows]
        for mask in middle[::-1]:
            for which, tail in enumerate(tails):
                keep, give, offset = [], [], 0
                for size in sizes:
                    keep.append(tail[offset : offset + size // 2])
                    give.append(tail[offset + size // 2 : offset + size])
                    offset += size
                tails[which] = jnp.concatenate(keep) + swap(jnp.concatenate(give), mask)
            sizes = [size // 2 for size in sizes]
        for mask in middle:
            features = features + swap(features, mask)
        came = swap(jnp.concatenate([features, tails[1]]), top)
        features = features + swap(features, low) + swap(features, low | top)
        features = (features + came[:cut]).reshape(lines, depth)
        tail = tails[0] + came[cut:]
        ends = [sum(sizes[: i + 1]) for i in range(len(sizes))]
        grad_b_up, grad_b_query, grad_b_value = [
            tail[end - size : end].reshape(-1) for end, size in zip(ends, sizes)
        ]
        grad_w_down, grad_w_up = totals[0][0], totals[1][0]
        grad_w_out, grad_w_query = jnp.split(totals[2][0], 2, axis=1)
        grad_w_key, grad_w_value = jnp.split(totals[3][0], 2, axis=1)
        mean_loss = features[4, 0] / (valid_count * depth)
        return (
            to_absolute(narrow(output)),
            mean_loss,
            to_absolute(grad_tokens),
            features[5],
            features[6],
            grad_w_query,
            grad_b_query,
            grad_w_key,
            grad_w_value,
            grad_b_value,
            grad_w_out,
            features[2],
            features[0],
            features[1],
            grad_w_up,
            grad_b_up,
            grad_w_down,
            features[3],
        )

    return body


def solution(mesh):
    placed = (
        P(("fsdp", "tp"), None),
        P(),
        P(),
        P("fsdp", "tp"),
        P("tp"),
        P("fsdp", "tp"),
        P("fsdp", "tp"),
        P("tp"),
        P("fsdp", "tp"),
        P(),
        P(),
        P(),
        P("fsdp", "tp"),
        P("tp"),
        P("fsdp", "tp"),
        P(),
        P(("fsdp", "tp"), None),
        P(("fsdp", "tp")),
        P("fsdp", None),
        P("fsdp", None, None),
    )
    return jax.shard_map(
        make_body(mesh.shape["fsdp"], mesh.shape["tp"]),
        mesh=mesh,
        in_specs=placed,
        out_specs=(
            P(("fsdp", "tp"), None),
            P(),
            P(("fsdp", "tp"), None),
            P(),
            P(),
            P("fsdp", "tp"),
            P("tp"),
            P("fsdp", "tp"),
            P("fsdp", "tp"),
            P("tp"),
            P("fsdp", "tp"),
            P(),
            P(),
            P(),
            P("fsdp", "tp"),
            P("tp"),
            P("fsdp", "tp"),
            P(),
        ),
        check_vma=False,
    )
```

```python
import jax
import jax.numpy as jnp
from jax import lax
from jax.experimental import pallas as pl
from jax.experimental.pallas import tpu as pltpu
from jax.sharding import PartitionSpec as P

HD = 64
PAIR = 2 * HD
EPSILON = 1e-05
MASKED_SCORE = -1e30
KEY_PAD = 128


def layer_norm(vectors, norm_gain, norm_shift):
    centre = jnp.mean(vectors, axis=-1, keepdims=True)
    centred = vectors - centre
    spread = jnp.mean(centred * centred, axis=-1, keepdims=True)
    return centred * lax.rsqrt(spread + EPSILON) * norm_gain + norm_shift


def contract(left_side, right_side, left_dim, right_dim):
    return lax.dot_general(
        left_side,
        right_side,
        (((left_dim,), (right_dim,)), ((), ())),
        preferred_element_type=jnp.float32,
    )


def narrow(values):
    return values.astype(jnp.bfloat16)


def after(values, *needed):
    return lax.optimization_barrier((values, needed))[0]


def bits_below(count, first):
    bits = []
    bit = first
    while bit < count:
        bits.append(bit)
        bit *= 2
    return bits


def segment_scores(q_ref, k_ref, ks_ref, seen_ref, row, seg, tree, place):
    rows = pl.ds(row, seg)
    lane = lax.broadcasted_iota(jnp.int32, (seg, PAIR), 1)
    first_head = lane < HD
    query = q_ref[rows, :]
    none = jnp.zeros_like(query)
    both = jnp.concatenate(
        [jnp.where(first_head, query, none), jnp.where(first_head, none, query)], axis=0
    )
    keys = jnp.concatenate([k_ref[rows, :], ks_ref[tree]], axis=0)
    scores = contract(both, keys, 1, 1)
    width = seg + KEY_PAD
    column = lax.broadcasted_iota(jnp.int32, (2 * seg, width), 1)
    position = lax.broadcasted_iota(jnp.int32, (2 * seg, width), 0)
    position = jnp.where(position >= seg, position - seg, position)
    seen = jnp.concatenate(
        [jnp.ones((1, seg), jnp.float32), seen_ref[pl.ds(place, 1), :]], axis=1
    )
    reach = jnp.where(column < seg, position, width)
    allowed = (column <= reach) & (seen > 0.5)
    scores = jnp.where(allowed, scores, MASKED_SCORE)
    highest = jnp.max(scores, axis=1, keepdims=True)
    raised = jnp.exp(scores - highest)
    probs = raised * (1.0 / jnp.sum(raised, axis=1, keepdims=True))
    return rows, first_head, both, keys, probs


def walk_segments(blocks, rows, seg, step):
    per = rows // seg
    for block in range(blocks):
        tree, far = block % 2, block // 2
        for inner in range(per):
            step(block * rows + inner * seg, tree, (tree * 2 + far) * per + inner)


def forward_kernel(rows, seg, q_ref, k_ref, v_ref, ks_ref, vs_ref, seen_ref, out_ref):
    def step(row, tree, place):
        at, first_head, both, keys, probs = segment_scores(
            q_ref, k_ref, ks_ref, seen_ref, row, seg, tree, place
        )
        values = jnp.concatenate([v_ref[at, :], vs_ref[tree]], axis=0)
        mixed = contract(narrow(probs), values, 1, 0)
        out_ref[at, :] = narrow(jnp.where(first_head, mixed[:seg], mixed[seg:]))

    walk_segments(4, rows, seg, step)


def backward_kernel(
    rows, seg, q_ref, k_ref, v_ref, go_ref, ks_ref, vs_ref, seen_ref, gq_ref, gk_ref, gv_ref, gks_ref, gvs_ref
):
    gks_ref[...] = jnp.zeros_like(gks_ref)
    gvs_ref[...] = jnp.zeros_like(gvs_ref)

    def step(row, tree, place):
        at, first_head, both, keys, probs = segment_scores(
            q_ref, k_ref, ks_ref, seen_ref, row, seg, tree, place
        )
        values = jnp.concatenate([v_ref[at, :], vs_ref[tree]], axis=0)
        grad_out = go_ref[at, :]
        none = jnp.zeros_like(grad_out)
        grad_both = jnp.concatenate(
            [jnp.where(first_head, grad_out, none), jnp.where(first_head, none, grad_out)], axis=0
        )
        grad_probs = contract(grad_both, values, 1, 1)
        inner = jnp.sum(probs * grad_probs, axis=1, keepdims=True)
        grad_scores = narrow(probs * (grad_probs - inner))
        grad_query = contract(grad_scores, keys, 1, 0)
        grad_query = narrow(jnp.where(first_head, grad_query[:seg], grad_query[seg:]))
        gq_ref[at, :] = grad_query * jnp.bfloat16(0.125)
        grad_keys = contract(grad_scores, both, 0, 0)
        gk_ref[at, :] = narrow(grad_keys[:seg])
        gks_ref[tree] += grad_keys[seg:]
        grad_values = contract(narrow(probs), grad_both, 0, 0)
        gv_ref[at, :] = narrow(grad_values[:seg])
        gvs_ref[tree] += grad_values[seg:]

    walk_segments(4, rows, seg, step)


def attend(kernel, rows, seg, operands, key_sums, seen, outputs, sums):
    count, width = operands[0].shape
    column_block = pl.BlockSpec((count, PAIR), lambda pair: (0, pair))
    sum_block = pl.BlockSpec((2, KEY_PAD, PAIR), lambda pair: (0, 0, pair))
    return pl.pallas_call(
        lambda *refs: kernel(rows, seg, *refs),
        grid=(width // PAIR,),
        in_specs=[column_block] * len(operands)
        + [sum_block] * 2
        + [pl.BlockSpec(seen.shape, lambda pair: (0, 0))],
        out_specs=[column_block] * outputs + [sum_block] * sums,
        out_shape=[jax.ShapeDtypeStruct((count, width), jnp.bfloat16)] * outputs
        + [jax.ShapeDtypeStruct((2, KEY_PAD, width), jnp.float32)] * sums,
        cost_estimate=pl.CostEstimate(flops=1, bytes_accessed=1, transcendentals=0),
        name="attend_forward" if sums == 0 else "attend_backward",
    )(*operands, *key_sums, seen)


def make_body(fsdp, tp):
    world = fsdp * tp
    low = 1
    top = tp // 2
    middle = bits_below(top, 2)
    mate = tp
    plane = bits_below(world, 2 * tp)

    def swap(values, mask):
        return lax.ppermute(values, ("fsdp", "tp"), [(i, i ^ mask) for i in range(world)])

    def body(
        tokens,
        norm1_gain,
        norm1_shift,
        w_query,
        b_query,
        w_key,
        w_value,
        b_value,
        w_out,
        b_out,
        norm2_gain,
        norm2_shift,
        w_up,
        b_up,
        w_down,
        b_down,
        teacher,
        valid_mask,
        parents,
        summary,
    ):
        rows, depth = tokens.shape
        strip = depth // fsdp
        half = depth // 2
        column = lax.axis_index("tp")
        device = lax.axis_index("fsdp")
        core = device % 2
        spot = device // 2
        upper = column // top
        alike = core == upper
        segments = parents.shape[1]
        marks = summary.shape[2]
        seg = rows * tp // segments
        per = rows // seg

        def mirrored(k):
            mirror, found = 0, 0
            for i in range(len(plane)):
                found = (k >> i) & 1
                mirror = mirror * 2 + found
            return mirror

        blocks = fsdp // 2

        def to_relative(values):
            parts = []
            for side in range(2):
                for k in range(blocks):
                    away = k if side == 0 else mirrored(k)
                    start = (2 * (spot ^ away) + side) * strip
                    parts.append(lax.dynamic_slice_in_dim(values, start, strip, values.ndim - 1))
            return jnp.concatenate(parts, axis=-1)

        def to_absolute(values):
            parts = []
            for place in range(blocks):
                away = spot ^ place
                back = jnp.zeros_like(away)
                for i in range(len(plane)):
                    back = back * 2 + ((away >> i) & 1)
                for side in range(2):
                    start = (away if side == 0 else blocks + back) * strip
                    parts.append(lax.dynamic_slice_in_dim(values, start, strip, values.ndim - 1))
            return jnp.concatenate(parts, axis=-1)

        lane = []
        gate = []
        sent = []

        def ship(items):
            values = after([value for value, _ in items], lane[-2:-1], gate)
            sent.append(values)
            got = [swap(value, mask) for value, (_, mask) in zip(values, items)]
            lane.append(got)
            return got

        orders = (plane, plane[::-1])
        slices = tp // 4

        def bring_weight(shard, across):
            mine = jnp.where(alike, shard, across)
            came = swap(jnp.where(alike, across, shard), mate)
            for mask in middle:
                mine = jnp.concatenate([mine, swap(mine, mask)], axis=1)
                came = jnp.concatenate([came, swap(came, mask)], axis=1)
            return [jnp.where(core == side, mine, came) for side in range(2)]

        def run(stages, *needed):
            gate[:] = needed
            next(stages, None)
            gate.clear()

        def finish(stages, *needed):
            gate[:] = needed
            for _ in stages:
                pass
            gate.clear()

        def gather_weight(both, full):
            sides = [[both[0]], [both[1]]]
            for level in range(len(plane)):
                held = [
                    pieces[0] if level == 0 else jnp.concatenate(pieces, axis=0) for pieces in sides
                ]
                got = ship([(held[side], orders[side][level]) for side in range(2)])
                yield
                got = after(got, gate)
                for side in range(2):
                    sides[side].append(got[side])
            full.append(jnp.concatenate(sides[0] + sides[1], axis=0))

        def scatter_weight(pairs, total, *ahead):
            def rows_of(start, stop, needed):
                parts = [
                    contract(after(left, needed)[:, start:stop], right, 0, 0) for left, right in pairs
                ]
                if len(parts) == 1:
                    return parts[0]
                parts = [part.reshape(stop - start, slices, -1) for part in parts]
                return jnp.concatenate(parts, axis=2).reshape(stop - start, -1)

            sums = []
            for level in reversed(range(len(plane))):
                size = half >> (len(plane) - level)
                if sums:
                    away = [narrow(sums[side][size:]) for side in range(2)]
                else:
                    away = [narrow(rows_of(side * half + size, (side + 1) * half, ahead)) for side in range(2)]
                got = ship([(away[side], orders[side][level]) for side in range(2)])
                yield
                got = after(got, gate)
                if sums:
                    sums = [sums[side][:size] + got[side] for side in range(2)]
                else:
                    sums = [rows_of(side * half, side * half + size, away) + got[side] for side in range(2)]
            kept = [narrow(sums[side]) for side in range(2)]
            mine = jnp.where(core == 0, kept[0], kept[1])
            other = jnp.where(core == 0, kept[1], kept[0])
            for mask in middle[::-1]:
                width = mine.shape[1] // 2
                mine = narrow(mine[:, :width].astype(jnp.float32) + swap(mine[:, width:], mask))
                other = narrow(other[:, :width].astype(jnp.float32) + swap(other[:, width:], mask))
            came = swap(other, mate)
            give = jnp.where(alike, came, mine)
            keep = jnp.where(alike, mine, came)
            given.append(give)
            total.append(keep.astype(jnp.float32) + swap(give, top))

        given = []

        def gather_bias(part):
            part = jnp.where(alike, part, swap(part, top))
            for mask in middle:
                part = jnp.concatenate([part, swap(part, mask)], axis=1)
            return part

        def spread_rows(own, *needed):
            across = after(swap(own, low), needed)
            near = jnp.concatenate([own, swap(own, mate)], axis=0)
            far = jnp.concatenate([across, swap(across, mate)], axis=0)
            return near, far

        def start_collect(values, partial):
            far_mate = swap(narrow(partial(row_block(values, 3))), mate)
            leaving = narrow(partial(row_block(values, 2)) + far_mate)
            crossing = swap(leaving, low)
            values = after(values, leaving)
            near_mate = swap(narrow(partial(row_block(values, 1))), mate)
            own = partial(row_block(values, 0))

            def complete(*needed):
                return own + near_mate + after(crossing, needed)

            return leaving, complete

        def row_block(values, block):
            return values[block * rows : (block + 1) * rows]

        inputs = to_relative(tokens).astype(jnp.float32)
        target = to_relative(teacher).astype(jnp.float32)
        vectors = to_relative(
            jnp.stack([norm1_gain, norm1_shift, b_out, norm2_gain, norm2_shift, b_down])
        )
        gain1, shift1, bias_out, gain2, shift2, bias_down = [vectors[i] for i in range(6)]
        weight_mask = valid_mask.astype(jnp.float32)[:, None]
        counted = jnp.full((8, 128), jnp.sum(weight_mask), jnp.float32)
        for mask in bits_below(world, tp):
            counted = counted + swap(counted, mask)
        counted = counted + sum(swap(counted, mask) for mask in range(1, tp))
        valid_count = counted[0, 0]

        shards = [
            jnp.concatenate([w_key, w_value], axis=1),
            jnp.concatenate([w_query, w_out], axis=1),
            w_up,
            w_down,
        ]
        crossed = []

        gathered = [[], [], [], []]

        leaving_shards = []

        def cross(which, *needed):
            leaving_shards.append(after(shards[which], needed))
            crossed.append(swap(leaving_shards[-1], top))

        def fetch(which, *needed):
            across = after(crossed[which], needed)
            return gather_weight(bring_weight(shards[which], across), gathered[which])

        cross(0)
        kv_stages = fetch(0, counted)
        run(kv_stages)
        cross(1, crossed[0])
        run(kv_stages)
        cross(2, lane[0])
        qo_stages = fetch(1, sent[-1])
        run(qo_stages)
        finish(kv_stages)
        run(qo_stages, crossed[2])
        up_stages = fetch(2, sent[-1])
        run(up_stages)
        cross(3, crossed[2])
        finish(qo_stages)
        w_kv, w_qo = gathered[0][0], gathered[1][0]

        def split_two(joined):
            parts = joined.reshape(joined.shape[0], slices, 2, -1)
            return [parts[:, :, i].reshape(joined.shape[0], -1) for i in range(2)]

        full_key, full_value = split_two(w_kv)
        full_query, full_out = split_two(w_qo)
        bias = gather_bias(jnp.concatenate([b_query, b_value, b_up])[None]).reshape(slices, -1)
        heads = b_query.shape[0]
        bias_query = bias[:, :heads].reshape(-1)
        bias_value = bias[:, heads : 2 * heads].reshape(-1)
        bias_up = bias[:, 2 * heads :].reshape(-1)

        tables = jnp.concatenate([parents[0][:, None], summary[0]], axis=1)
        tables = jnp.stack([tables, swap(tables, mate)])
        seg_ids = jnp.arange(segments, dtype=jnp.int32)
        moved = seg_ids ^ (column * per)
        picks = moved[:, None] == seg_ids[None, :]
        tables = jnp.sum(jnp.where(picks[None, :, :, None], tables[:, None], 0), axis=2)
        parent_rel = jnp.where(tables[:, :, 0] >= 0, tables[:, :, 0] ^ (column * per), -1)
        offsets_rel = tables[:, :, 1:]
        reach = (parent_rel[:, :, None] == seg_ids[None, None, :]).astype(jnp.float32)
        unit = (seg_ids[:, None] == seg_ids[None, :]).astype(jnp.float32)[None]
        closure = reach + unit
        steps = 1
        while steps < segments:
            closure = jnp.einsum("tij,tjk->tik", closure, closure)
            closure = jnp.minimum(closure, 1.0)
            steps *= 2
        closure = closure - unit
        local = 2 * per
        seen = jnp.repeat(closure[:, :local], marks, axis=2)
        seen = jnp.pad(seen, ((0, 0), (0, 0), (0, KEY_PAD - segments * marks)))
        seen = seen.reshape(2 * local, KEY_PAD)
        far_id = jnp.arange(local, dtype=jnp.int32) // per
        inner_id = jnp.arange(local, dtype=jnp.int32) % per
        tree_id = jnp.arange(2, dtype=jnp.int32)
        start = (far_id[None, :] * 2 + tree_id[:, None]) * rows + inner_id[None, :] * seg
        summary_row = (start[:, :, None] + offsets_rel[:, :local]).reshape(-1)
        chosen = narrow(summary_row[:, None] == jnp.arange(4 * rows, dtype=jnp.int32)[None, :])

        def spread_sums(part, needed):
            for mask in middle + [top]:
                part = jnp.concatenate([part, after(swap(part, mask), needed)], axis=1)
            return jnp.pad(part, ((0, 0), (0, KEY_PAD - part.shape[1]), (0, 0)))

        def collect_sums(whole, *needed):
            whole = whole[:, : segments * marks]
            for mask in [top] + middle[::-1]:
                size = whole.shape[1] // 2
                whole = whole[:, :size] + after(swap(narrow(whole[:, size:]), mask), needed)
            return whole

        normed = narrow(layer_norm(inputs, gain1, shift1))
        normed_near, normed_far = spread_rows(after(normed, crossed[0], bias, tables))
        normed_all = jnp.concatenate([normed_near, normed_far], axis=0)
        key_states = narrow(contract(normed_all, full_key, 1, 0))
        value_states = narrow(contract(normed_all, full_value, 1, 0) + bias_value)
        queries = narrow((contract(normed_all, full_query, 1, 0) + bias_query) * 0.125)
        width = queries.shape[1]
        picked = jnp.concatenate(
            [narrow(contract(chosen, key_states, 1, 0)), narrow(contract(chosen, value_states, 1, 0))],
            axis=1,
        )
        picked = picked.reshape(2, local * marks, 2 * width)
        run(up_stages)
        down_stages = fetch(3, sent[-1])
        run(down_stages)
        queries, normed_all = after((queries, normed_all), sent[-1])
        up_came = lane[-2]
        picked = spread_sums(picked, queries)
        key_sums = (picked[:, :, :width], picked[:, :, width:])
        (attended,) = attend(
            forward_kernel, rows, seg, (queries, key_states, value_states), key_sums, seen, 1, 0
        )
        leaving, complete = start_collect(after(attended, up_came), lambda block: contract(block, full_out, 1, 1))
        run(down_stages, leaving)
        branch = complete(sent[-1])
        hidden = inputs + branch + bias_out

        normed_mid = narrow(layer_norm(hidden, gain2, shift2))
        finish(up_stages, normed_mid)
        mid_near, mid_far = spread_rows(normed_mid)
        full_up = gathered[2][0]
        active = []
        for part in (mid_near, mid_far):
            part = after(part, active)
            active.append(narrow(jnp.maximum(contract(part, full_up, 1, 0) + bias_up, 0.0)))
        finish(down_stages)
        full_down = gathered[3][0]
        active_all = jnp.concatenate(active, axis=0)
        mid_all = jnp.concatenate([mid_near, mid_far], axis=0)
        _, complete = start_collect(active_all, lambda block: contract(block, full_down, 1, 1))
        feed_out = complete()
        output = hidden + feed_out + bias_down

        deviation = output - target
        squares = jnp.sum(weight_mask * deviation * deviation)
        total_tokens = rows * world
        grad_output = (2.0 * total_tokens / valid_count) * weight_mask * deviation

        feed_near, feed_far = spread_rows(narrow(grad_output))
        feed_all = jnp.concatenate([feed_near, feed_far], axis=0)
        totals = [[], [], [], []]
        down_stages = scatter_weight([(feed_all, active_all)], totals[0])
        run(down_stages)
        feed_near, feed_far = after((feed_near, feed_far), sent[-1])
        grad_pre = []
        for part, kept in zip((feed_near, feed_far), active):
            part = after(part, grad_pre)
            grad_pre.append(narrow(jnp.where(kept > 0, contract(part, full_down, 1, 0), 0.0)))
        grad_pre_all = jnp.concatenate(grad_pre, axis=0)
        mid_leaving, complete = start_collect(grad_pre_all, lambda block: contract(block, full_up, 1, 1))
        up_stages = scatter_weight([(mid_all, grad_pre_all)], totals[1], mid_leaving)
        run(up_stages)
        run(down_stages, sent[-1])
        grad_mid = complete(sent[-1])
        second_norm, second_pull = jax.vjp(layer_norm, hidden, gain2, shift2)
        grad_hidden_norm, grad_gain2, grad_shift2 = second_pull(grad_mid)
        grad_hidden = grad_output + grad_hidden_norm

        grad_branch = narrow(grad_hidden)
        branch_near, branch_far = spread_rows(grad_branch)
        run(up_stages, grad_branch)
        finish(down_stages, sent[-1])
        branch_far = after(branch_far, given[0])
        branch_all = jnp.concatenate([branch_near, branch_far], axis=0)
        grad_attended = narrow(contract(branch_all, full_out, 1, 0))
        grad_pre_query, grad_keys, grad_values, key_part, value_part = attend(
            backward_kernel,
            rows,
            seg,
            (queries, key_states, value_states, grad_attended),
            key_sums,
            seen,
            3,
            2,
        )
        first_stages = scatter_weight(
            [(branch_all, attended), (normed_all, grad_pre_query)], totals[2], grad_pre_query
        )
        run(first_stages)
        finish(up_stages, sent[-1])
        key_part, value_part = after((key_part, value_part), sent[-1])
        parts = collect_sums(jnp.concatenate([key_part, value_part], axis=2), given[1], totals[0])
        parts = narrow(parts.reshape(-1, 2 * width))
        grad_keys = narrow(grad_keys + contract(chosen, parts[:, :width], 0, 0))
        grad_values = narrow(grad_values + contract(chosen, parts[:, width:], 0, 0))
        joined_grads = jnp.concatenate([grad_keys, grad_values, grad_pre_query], axis=1)

        def normed_part(block):
            return (
                contract(block[:, :width], full_key, 1, 1)
                + contract(block[:, width : 2 * width], full_value, 1, 1)
                + contract(block[:, 2 * width :], full_query, 1, 1)
            )

        normed_leaving, complete = start_collect(joined_grads, normed_part)
        last_stages = scatter_weight(
            [(normed_all, grad_keys), (normed_all, grad_values)], totals[3], normed_leaving
        )
        run(last_stages)
        late = sent[-1]
        grad_normed = complete(late)
        run(first_stages, given[1])
        run(last_stages, totals[1])
        finish(first_stages, late)
        finish(last_stages)
        first_norm, first_pull = jax.vjp(layer_norm, inputs, gain1, shift1)
        grad_input_norm, grad_gain1, grad_shift1 = first_pull(grad_normed)
        grad_tokens = grad_hidden + grad_input_norm

        feature_rows = [
            grad_gain2,
            grad_shift2,
            jnp.sum(grad_hidden, axis=0),
            jnp.sum(grad_output, axis=0),
            jnp.full((depth,), squares, jnp.float32),
            grad_gain1,
            grad_shift1,
        ]
        head_rows = [
            jnp.sum(grad_pre_all.astype(jnp.float32), axis=0),
            jnp.sum(grad_pre_query.astype(jnp.float32), axis=0),
            jnp.sum(grad_values.astype(jnp.float32), axis=0),
        ]
        lines = len(feature_rows)
        cut = lines * depth // 128
        joined = to_absolute(jnp.stack(feature_rows)).reshape(-1, 128)
        joined = jnp.concatenate([joined] + [v.reshape(-1, 128) for v in head_rows])
        for mask in plane:
            joined = joined + after(swap(joined, mask), lane[-1] if mask == plane[-1] else sent[-1])
        came = swap(joined, mate)
        features = joined[:cut] + came[:cut]
        tails = [jnp.where(alike, joined[cut:], came[cut:]), jnp.where(alike, came[cut:], joined[cut:])]
        sizes = [v.shape[0] // 128 for v in head_rows]
        for mask in middle[::-1]:
            for which, tail in enumerate(tails):
                keep, give, offset = [], [], 0
                for size in sizes:
                    keep.append(tail[offset : offset + size // 2])
                    give.append(tail[offset + size // 2 : offset + size])
                    offset += size
                tails[which] = jnp.concatenate(keep) + swap(jnp.concatenate(give), mask)
            sizes = [size // 2 for size in sizes]
        for mask in middle:
            features = features + swap(features, mask)
        features, tails = after((features, tails), given[3])
        came = swap(jnp.concatenate([features, tails[1]]), top)
        features = features + swap(features, low) + swap(features, low | top)
        features = (features + came[:cut]).reshape(lines, depth)
        tail = tails[0] + came[cut:]
        ends = [sum(sizes[: i + 1]) for i in range(len(sizes))]
        grad_b_up, grad_b_query, grad_b_value = [
            tail[end - size : end].reshape(-1) for end, size in zip(ends, sizes)
        ]
        grad_w_down, grad_w_up = totals[0][0], totals[1][0]
        grad_w_out, grad_w_query = jnp.split(totals[2][0], 2, axis=1)
        grad_w_key, grad_w_value = jnp.split(totals[3][0], 2, axis=1)
        mean_loss = features[4, 0] / (valid_count * depth)
        return (
            to_absolute(narrow(output)),
            mean_loss,
            to_absolute(grad_tokens),
            features[5],
            features[6],
            grad_w_query,
            grad_b_query,
            grad_w_key,
            grad_w_value,
            grad_b_value,
            grad_w_out,
            features[2],
            features[0],
            features[1],
            grad_w_up,
            grad_b_up,
            grad_w_down,
            features[3],
        )

    return body


def solution(mesh):
    placed = (
        P(("fsdp", "tp"), None),
        P(),
        P(),
        P("fsdp", "tp"),
        P("tp"),
        P("fsdp", "tp"),
        P("fsdp", "tp"),
        P("tp"),
        P("fsdp", "tp"),
        P(),
        P(),
        P(),
        P("fsdp", "tp"),
        P("tp"),
        P("fsdp", "tp"),
        P(),
        P(("fsdp", "tp"), None),
        P(("fsdp", "tp")),
        P("fsdp", None),
        P("fsdp", None, None),
    )
    return jax.shard_map(
        make_body(mesh.shape["fsdp"], mesh.shape["tp"]),
        mesh=mesh,
        in_specs=placed,
        out_specs=(
            P(("fsdp", "tp"), None),
            P(),
            P(("fsdp", "tp"), None),
            P(),
            P(),
            P("fsdp", "tp"),
            P("tp"),
            P("fsdp", "tp"),
            P("fsdp", "tp"),
            P("tp"),
            P("fsdp", "tp"),
            P(),
            P(),
            P(),
            P("fsdp", "tp"),
            P("tp"),
            P("fsdp", "tp"),
            P(),
        ),
        check_vma=False,
    )
```

```python
import jax
import jax.numpy as jnp
from jax import lax
from jax.experimental import pallas as pl
from jax.experimental.pallas import tpu as pltpu
from jax.sharding import PartitionSpec as P

HD = 64
PAIR = 2 * HD
EPSILON = 1e-05
MASKED_SCORE = -1e30
KEY_PAD = 128


def layer_norm(vectors, norm_gain, norm_shift):
    centre = jnp.mean(vectors, axis=-1, keepdims=True)
    centred = vectors - centre
    spread = jnp.mean(centred * centred, axis=-1, keepdims=True)
    return centred * lax.rsqrt(spread + EPSILON) * norm_gain + norm_shift


def contract(left_side, right_side, left_dim, right_dim):
    return lax.dot_general(
        left_side,
        right_side,
        (((left_dim,), (right_dim,)), ((), ())),
        preferred_element_type=jnp.float32,
    )


def narrow(values):
    return values.astype(jnp.bfloat16)


def after(values, *needed):
    return lax.optimization_barrier((values, needed))[0]


def bits_below(count, first):
    bits = []
    bit = first
    while bit < count:
        bits.append(bit)
        bit *= 2
    return bits


def segment_scores(q_ref, k_ref, ks_ref, seen_ref, row, seg, tree, place):
    rows = pl.ds(row, seg)
    lane = lax.broadcasted_iota(jnp.int32, (seg, PAIR), 1)
    first_head = lane < HD
    query = q_ref[rows, :]
    none = jnp.zeros_like(query)
    both = jnp.concatenate(
        [jnp.where(first_head, query, none), jnp.where(first_head, none, query)], axis=0
    )
    keys = jnp.concatenate([k_ref[rows, :], ks_ref[tree]], axis=0)
    scores = contract(both, keys, 1, 1)
    width = seg + KEY_PAD
    column = lax.broadcasted_iota(jnp.int32, (2 * seg, width), 1)
    position = lax.broadcasted_iota(jnp.int32, (2 * seg, width), 0)
    position = jnp.where(position >= seg, position - seg, position)
    seen = jnp.concatenate(
        [jnp.ones((1, seg), jnp.float32), seen_ref[pl.ds(place, 1), :]], axis=1
    )
    reach = jnp.where(column < seg, position, width)
    allowed = (column <= reach) & (seen > 0.5)
    scores = jnp.where(allowed, scores, MASKED_SCORE)
    highest = jnp.max(scores, axis=1, keepdims=True)
    raised = jnp.exp(scores - highest)
    probs = raised * (1.0 / jnp.sum(raised, axis=1, keepdims=True))
    return rows, first_head, both, keys, probs


def walk_segments(blocks, rows, seg, step):
    per = rows // seg
    for block in range(blocks):
        tree, far = block % 2, block // 2
        for inner in range(per):
            step(block * rows + inner * seg, tree, (tree * 2 + far) * per + inner)


def forward_kernel(rows, seg, q_ref, k_ref, v_ref, ks_ref, vs_ref, seen_ref, out_ref):
    def step(row, tree, place):
        at, first_head, both, keys, probs = segment_scores(
            q_ref, k_ref, ks_ref, seen_ref, row, seg, tree, place
        )
        values = jnp.concatenate([v_ref[at, :], vs_ref[tree]], axis=0)
        mixed = contract(narrow(probs), values, 1, 0)
        out_ref[at, :] = narrow(jnp.where(first_head, mixed[:seg], mixed[seg:]))

    walk_segments(4, rows, seg, step)


def backward_kernel(
    rows, seg, q_ref, k_ref, v_ref, go_ref, ks_ref, vs_ref, seen_ref, gq_ref, gk_ref, gv_ref, gks_ref, gvs_ref
):
    gks_ref[...] = jnp.zeros_like(gks_ref)
    gvs_ref[...] = jnp.zeros_like(gvs_ref)

    def step(row, tree, place):
        at, first_head, both, keys, probs = segment_scores(
            q_ref, k_ref, ks_ref, seen_ref, row, seg, tree, place
        )
        values = jnp.concatenate([v_ref[at, :], vs_ref[tree]], axis=0)
        grad_out = go_ref[at, :]
        none = jnp.zeros_like(grad_out)
        grad_both = jnp.concatenate(
            [jnp.where(first_head, grad_out, none), jnp.where(first_head, none, grad_out)], axis=0
        )
        grad_probs = contract(grad_both, values, 1, 1)
        inner = jnp.sum(probs * grad_probs, axis=1, keepdims=True)
        grad_scores = narrow(probs * (grad_probs - inner))
        grad_query = contract(grad_scores, keys, 1, 0)
        grad_query = narrow(jnp.where(first_head, grad_query[:seg], grad_query[seg:]))
        gq_ref[at, :] = grad_query * jnp.bfloat16(0.125)
        grad_keys = contract(grad_scores, both, 0, 0)
        gk_ref[at, :] = narrow(grad_keys[:seg])
        gks_ref[tree] += grad_keys[seg:]
        grad_values = contract(narrow(probs), grad_both, 0, 0)
        gv_ref[at, :] = narrow(grad_values[:seg])
        gvs_ref[tree] += grad_values[seg:]

    walk_segments(4, rows, seg, step)


def attend(kernel, rows, seg, operands, key_sums, seen, outputs, sums):
    count, width = operands[0].shape
    column_block = pl.BlockSpec((count, PAIR), lambda pair: (0, pair))
    sum_block = pl.BlockSpec((2, KEY_PAD, PAIR), lambda pair: (0, 0, pair))
    return pl.pallas_call(
        lambda *refs: kernel(rows, seg, *refs),
        grid=(width // PAIR,),
        in_specs=[column_block] * len(operands)
        + [sum_block] * 2
        + [pl.BlockSpec(seen.shape, lambda pair: (0, 0))],
        out_specs=[column_block] * outputs + [sum_block] * sums,
        out_shape=[jax.ShapeDtypeStruct((count, width), jnp.bfloat16)] * outputs
        + [jax.ShapeDtypeStruct((2, KEY_PAD, width), jnp.float32)] * sums,
        cost_estimate=pl.CostEstimate(flops=1, bytes_accessed=1, transcendentals=0),
        name="attend_forward" if sums == 0 else "attend_backward",
    )(*operands, *key_sums, seen)


def make_body(fsdp, tp):
    world = fsdp * tp
    low = 1
    top = tp // 2
    middle = bits_below(top, 2)
    mate = tp
    plane = bits_below(world, 2 * tp)

    def swap(values, mask):
        return lax.ppermute(values, ("fsdp", "tp"), [(i, i ^ mask) for i in range(world)])

    def body(
        tokens,
        norm1_gain,
        norm1_shift,
        w_query,
        b_query,
        w_key,
        w_value,
        b_value,
        w_out,
        b_out,
        norm2_gain,
        norm2_shift,
        w_up,
        b_up,
        w_down,
        b_down,
        teacher,
        valid_mask,
        parents,
        summary,
    ):
        rows, depth = tokens.shape
        strip = depth // fsdp
        half = depth // 2
        column = lax.axis_index("tp")
        device = lax.axis_index("fsdp")
        core = device % 2
        spot = device // 2
        upper = column // top
        alike = core == upper
        segments = parents.shape[1]
        marks = summary.shape[2]
        seg = rows * tp // segments
        per = rows // seg

        def mirrored(k):
            mirror, found = 0, 0
            for i in range(len(plane)):
                found = (k >> i) & 1
                mirror = mirror * 2 + found
            return mirror

        blocks = fsdp // 2

        def to_relative(values):
            parts = []
            for side in range(2):
                for k in range(blocks):
                    away = k if side == 0 else mirrored(k)
                    start = (2 * (spot ^ away) + side) * strip
                    parts.append(lax.dynamic_slice_in_dim(values, start, strip, values.ndim - 1))
            return jnp.concatenate(parts, axis=-1)

        def to_absolute(values):
            parts = []
            for place in range(blocks):
                away = spot ^ place
                back = jnp.zeros_like(away)
                for i in range(len(plane)):
                    back = back * 2 + ((away >> i) & 1)
                for side in range(2):
                    start = (away if side == 0 else blocks + back) * strip
                    parts.append(lax.dynamic_slice_in_dim(values, start, strip, values.ndim - 1))
            return jnp.concatenate(parts, axis=-1)

        lane = []
        gate = []
        sent = []

        def ship(items):
            values = after([value for value, _ in items], lane[-2:-1], gate)
            sent.append(values)
            got = [swap(value, mask) for value, (_, mask) in zip(values, items)]
            lane.append(got)
            return got

        orders = (plane, plane[::-1])
        slices = tp // 4

        def bring_weight(shard, across):
            mine = jnp.where(alike, shard, across)
            came = swap(jnp.where(alike, across, shard), mate)
            for mask in middle:
                mine = jnp.concatenate([mine, swap(mine, mask)], axis=1)
                came = jnp.concatenate([came, swap(came, mask)], axis=1)
            return [jnp.where(core == side, mine, came) for side in range(2)]

        def run(stages, *needed):
            gate[:] = needed
            next(stages, None)
            gate.clear()

        def finish(stages, *needed):
            gate[:] = needed
            for _ in stages:
                pass
            gate.clear()

        def gather_weight(both, full):
            sides = [[both[0]], [both[1]]]
            for level in range(len(plane)):
                held = [
                    pieces[0] if level == 0 else jnp.concatenate(pieces, axis=0) for pieces in sides
                ]
                got = ship([(held[side], orders[side][level]) for side in range(2)])
                yield
                got = after(got, gate)
                for side in range(2):
                    sides[side].append(got[side])
            full.append(jnp.concatenate(sides[0] + sides[1], axis=0))

        def scatter_weight(pairs, total, *ahead):
            def rows_of(start, stop, needed):
                parts = [
                    contract(after(left, needed)[:, start:stop], right, 0, 0) for left, right in pairs
                ]
                if len(parts) == 1:
                    return parts[0]
                parts = [part.reshape(stop - start, slices, -1) for part in parts]
                return jnp.concatenate(parts, axis=2).reshape(stop - start, -1)

            sums = []
            for level in reversed(range(len(plane))):
                size = half >> (len(plane) - level)
                if sums:
                    away = [narrow(sums[side][size:]) for side in range(2)]
                else:
                    away = [narrow(rows_of(side * half + size, (side + 1) * half, ahead)) for side in range(2)]
                got = ship([(away[side], orders[side][level]) for side in range(2)])
                yield
                got = after(got, gate)
                if sums:
                    sums = [sums[side][:size] + got[side] for side in range(2)]
                else:
                    sums = [rows_of(side * half, side * half + size, away) + got[side] for side in range(2)]
            kept = [narrow(sums[side]) for side in range(2)]
            mine = jnp.where(core == 0, kept[0], kept[1])
            other = jnp.where(core == 0, kept[1], kept[0])
            for mask in middle[::-1]:
                width = mine.shape[1] // 2
                mine = narrow(mine[:, :width].astype(jnp.float32) + swap(mine[:, width:], mask))
                other = narrow(other[:, :width].astype(jnp.float32) + swap(other[:, width:], mask))
            came = swap(other, mate)
            give = jnp.where(alike, came, mine)
            keep = jnp.where(alike, mine, came)
            given.append(give)
            total.append(keep.astype(jnp.float32) + swap(give, top))

        given = []

        def gather_bias(part):
            part = jnp.where(alike, part, swap(part, top))
            for mask in middle:
                part = jnp.concatenate([part, swap(part, mask)], axis=1)
            return part

        def spread_rows(own, *needed):
            across = after(swap(own, low), needed)
            near = jnp.concatenate([own, swap(own, mate)], axis=0)
            far = jnp.concatenate([across, swap(across, mate)], axis=0)
            return near, far

        def start_collect(values, partial):
            far_mate = swap(narrow(partial(row_block(values, 3))), mate)
            leaving = narrow(partial(row_block(values, 2)) + far_mate)
            crossing = swap(leaving, low)
            values = after(values, leaving)
            near_mate = swap(narrow(partial(row_block(values, 1))), mate)
            own = partial(row_block(values, 0))

            def complete(*needed):
                return own + near_mate + after(crossing, needed)

            return leaving, complete

        def row_block(values, block):
            return values[block * rows : (block + 1) * rows]

        inputs = to_relative(tokens).astype(jnp.float32)
        target = to_relative(teacher).astype(jnp.float32)
        vectors = to_relative(
            jnp.stack([norm1_gain, norm1_shift, b_out, norm2_gain, norm2_shift, b_down])
        )
        gain1, shift1, bias_out, gain2, shift2, bias_down = [vectors[i] for i in range(6)]
        weight_mask = valid_mask.astype(jnp.float32)[:, None]
        counted = jnp.full((8, 128), jnp.sum(weight_mask), jnp.float32)
        for mask in bits_below(world, tp):
            counted = counted + swap(counted, mask)
        counted = counted + sum(swap(counted, mask) for mask in range(1, tp))
        valid_count = counted[0, 0]

        shards = [
            jnp.concatenate([w_key, w_value], axis=1),
            jnp.concatenate([w_query, w_out], axis=1),
            w_up,
            w_down,
        ]
        crossed = []

        gathered = [[], [], [], []]

        leaving_shards = []

        def cross(which, *needed):
            leaving_shards.append(after(shards[which], needed))
            crossed.append(swap(leaving_shards[-1], top))

        def fetch(which, *needed):
            across = after(crossed[which], needed)
            return gather_weight(bring_weight(shards[which], across), gathered[which])

        cross(0)
        kv_stages = fetch(0, counted)
        run(kv_stages)
        cross(1, crossed[0])
        run(kv_stages)
        cross(2, lane[0])
        qo_stages = fetch(1, sent[-1])
        run(qo_stages)
        finish(kv_stages)
        run(qo_stages, crossed[2])
        up_stages = fetch(2, sent[-1])
        run(up_stages)
        cross(3, crossed[2])
        finish(qo_stages)
        w_kv, w_qo = gathered[0][0], gathered[1][0]

        def split_two(joined):
            parts = joined.reshape(joined.shape[0], slices, 2, -1)
            return [parts[:, :, i].reshape(joined.shape[0], -1) for i in range(2)]

        full_key, full_value = split_two(w_kv)
        full_query, full_out = split_two(w_qo)
        bias = gather_bias(jnp.concatenate([b_query, b_value, b_up])[None]).reshape(slices, -1)
        heads = b_query.shape[0]
        bias_query = bias[:, :heads].reshape(-1)
        bias_value = bias[:, heads : 2 * heads].reshape(-1)
        bias_up = bias[:, 2 * heads :].reshape(-1)

        tables = jnp.concatenate([parents[0][:, None], summary[0]], axis=1)
        tables = jnp.stack([tables, swap(tables, mate)])
        seg_ids = jnp.arange(segments, dtype=jnp.int32)
        moved = seg_ids ^ (column * per)
        picks = moved[:, None] == seg_ids[None, :]
        tables = jnp.sum(jnp.where(picks[None, :, :, None], tables[:, None], 0), axis=2)
        parent_rel = jnp.where(tables[:, :, 0] >= 0, tables[:, :, 0] ^ (column * per), -1)
        offsets_rel = tables[:, :, 1:]
        reach = (parent_rel[:, :, None] == seg_ids[None, None, :]).astype(jnp.float32)
        unit = (seg_ids[:, None] == seg_ids[None, :]).astype(jnp.float32)[None]
        closure = reach + unit
        steps = 1
        while steps < segments:
            closure = jnp.einsum("tij,tjk->tik", closure, closure)
            closure = jnp.minimum(closure, 1.0)
            steps *= 2
        closure = closure - unit
        local = 2 * per
        seen = jnp.repeat(closure[:, :local], marks, axis=2)
        seen = jnp.pad(seen, ((0, 0), (0, 0), (0, KEY_PAD - segments * marks)))
        seen = seen.reshape(2 * local, KEY_PAD)
        far_id = jnp.arange(local, dtype=jnp.int32) // per
        inner_id = jnp.arange(local, dtype=jnp.int32) % per
        tree_id = jnp.arange(2, dtype=jnp.int32)
        start = (far_id[None, :] * 2 + tree_id[:, None]) * rows + inner_id[None, :] * seg
        summary_row = (start[:, :, None] + offsets_rel[:, :local]).reshape(-1)
        chosen = narrow(summary_row[:, None] == jnp.arange(4 * rows, dtype=jnp.int32)[None, :])

        def spread_sums(part, needed):
            for mask in middle + [top]:
                part = jnp.concatenate([part, after(swap(part, mask), needed)], axis=1)
            return jnp.pad(part, ((0, 0), (0, KEY_PAD - part.shape[1]), (0, 0)))

        def collect_sums(whole, *needed):
            whole = whole[:, : segments * marks]
            for mask in [top] + middle[::-1]:
                size = whole.shape[1] // 2
                whole = whole[:, :size] + after(swap(narrow(whole[:, size:]), mask), needed)
            return whole

        normed = narrow(layer_norm(inputs, gain1, shift1))
        normed_near, normed_far = spread_rows(after(normed, crossed[0], bias, tables))
        normed_all = jnp.concatenate([normed_near, normed_far], axis=0)
        key_states = narrow(contract(normed_all, full_key, 1, 0))
        value_states = narrow(contract(normed_all, full_value, 1, 0) + bias_value)
        queries = narrow((contract(normed_all, full_query, 1, 0) + bias_query) * 0.125)
        width = queries.shape[1]
        picked = jnp.concatenate(
            [narrow(contract(chosen, key_states, 1, 0)), narrow(contract(chosen, value_states, 1, 0))],
            axis=1,
        )
        picked = picked.reshape(2, local * marks, 2 * width)
        run(up_stages)
        down_stages = fetch(3, sent[-1])
        run(down_stages)
        queries, normed_all = after((queries, normed_all), sent[-1])
        up_came = lane[-2]
        picked = spread_sums(picked, queries)
        key_sums = (picked[:, :, :width], picked[:, :, width:])
        (attended,) = attend(
            forward_kernel, rows, seg, (queries, key_states, value_states), key_sums, seen, 1, 0
        )
        leaving, complete = start_collect(after(attended, up_came), lambda block: contract(block, full_out, 1, 1))
        run(down_stages, leaving)
        branch = complete(sent[-1])
        hidden = inputs + branch + bias_out

        normed_mid = narrow(layer_norm(hidden, gain2, shift2))
        finish(up_stages, normed_mid)
        mid_near, mid_far = spread_rows(normed_mid)
        full_up = gathered[2][0]
        active = []
        for part in (mid_near, mid_far):
            part = after(part, active)
            active.append(narrow(jnp.maximum(contract(part, full_up, 1, 0) + bias_up, 0.0)))
        finish(down_stages, active)
        full_down = gathered[3][0]
        active_all = jnp.concatenate(active, axis=0)
        mid_all = jnp.concatenate([mid_near, mid_far], axis=0)
        _, complete = start_collect(active_all, lambda block: contract(block, full_down, 1, 1))
        feed_out = complete()
        output = hidden + feed_out + bias_down

        deviation = output - target
        squares = jnp.sum(weight_mask * deviation * deviation)
        total_tokens = rows * world
        grad_output = (2.0 * total_tokens / valid_count) * weight_mask * deviation

        feed_near, feed_far = spread_rows(narrow(grad_output))
        feed_all = jnp.concatenate([feed_near, feed_far], axis=0)
        totals = [[], [], [], []]
        down_stages = scatter_weight([(feed_all, active_all)], totals[0])
        run(down_stages)
        feed_near, feed_far = after((feed_near, feed_far), sent[-1])
        grad_pre = []
        for part, kept in zip((feed_near, feed_far), active):
            part = after(part, grad_pre)
            grad_pre.append(narrow(jnp.where(kept > 0, contract(part, full_down, 1, 0), 0.0)))
        grad_pre_all = jnp.concatenate(grad_pre, axis=0)
        mid_leaving, complete = start_collect(grad_pre_all, lambda block: contract(block, full_up, 1, 1))
        up_stages = scatter_weight([(mid_all, grad_pre_all)], totals[1], mid_leaving)
        run(up_stages)
        run(down_stages, sent[-1])
        grad_mid = complete(sent[-1])
        second_norm, second_pull = jax.vjp(layer_norm, hidden, gain2, shift2)
        grad_hidden_norm, grad_gain2, grad_shift2 = second_pull(grad_mid)
        grad_hidden = grad_output + grad_hidden_norm

        grad_branch = narrow(grad_hidden)
        branch_near, branch_far = spread_rows(grad_branch)
        run(up_stages, grad_branch)
        finish(down_stages, sent[-1])
        branch_far = after(branch_far, given[0])
        branch_all = jnp.concatenate([branch_near, branch_far], axis=0)
        grad_attended = narrow(contract(branch_all, full_out, 1, 0))
        grad_pre_query, grad_keys, grad_values, key_part, value_part = attend(
            backward_kernel,
            rows,
            seg,
            (queries, key_states, value_states, grad_attended),
            key_sums,
            seen,
            3,
            2,
        )
        first_stages = scatter_weight(
            [(branch_all, attended), (normed_all, grad_pre_query)], totals[2], grad_pre_query
        )
        run(first_stages)
        finish(up_stages, sent[-1])
        key_part, value_part = after((key_part, value_part), sent[-1])
        parts = collect_sums(jnp.concatenate([key_part, value_part], axis=2), given[1], totals[0])
        parts = narrow(parts.reshape(-1, 2 * width))
        grad_keys = narrow(grad_keys + contract(chosen, parts[:, :width], 0, 0))
        grad_values = narrow(grad_values + contract(chosen, parts[:, width:], 0, 0))
        joined_grads = jnp.concatenate([grad_keys, grad_values, grad_pre_query], axis=1)

        def normed_part(block):
            return (
                contract(block[:, :width], full_key, 1, 1)
                + contract(block[:, width : 2 * width], full_value, 1, 1)
                + contract(block[:, 2 * width :], full_query, 1, 1)
            )

        normed_leaving, complete = start_collect(joined_grads, normed_part)
        last_stages = scatter_weight(
            [(normed_all, grad_keys), (normed_all, grad_values)], totals[3], normed_leaving
        )
        run(last_stages)
        late = sent[-1]
        grad_normed = complete(late)
        run(first_stages, given[1])
        run(last_stages, totals[1])
        finish(first_stages, late)
        finish(last_stages)
        first_norm, first_pull = jax.vjp(layer_norm, inputs, gain1, shift1)
        grad_input_norm, grad_gain1, grad_shift1 = first_pull(grad_normed)
        grad_tokens = grad_hidden + grad_input_norm

        feature_rows = [
            grad_gain2,
            grad_shift2,
            jnp.sum(grad_hidden, axis=0),
            jnp.sum(grad_output, axis=0),
            jnp.full((depth,), squares, jnp.float32),
            grad_gain1,
            grad_shift1,
        ]
        head_rows = [
            jnp.sum(grad_pre_all.astype(jnp.float32), axis=0),
            jnp.sum(grad_pre_query.astype(jnp.float32), axis=0),
            jnp.sum(grad_values.astype(jnp.float32), axis=0),
        ]
        lines = len(feature_rows)
        cut = lines * depth // 128
        joined = to_absolute(jnp.stack(feature_rows)).reshape(-1, 128)
        joined = jnp.concatenate([joined] + [v.reshape(-1, 128) for v in head_rows])
        for mask in plane:
            joined = joined + after(swap(joined, mask), lane[-1] if mask == plane[-1] else sent[-1])
        came = swap(joined, mate)
        features = joined[:cut] + came[:cut]
        tails = [jnp.where(alike, joined[cut:], came[cut:]), jnp.where(alike, came[cut:], joined[cut:])]
        sizes = [v.shape[0] // 128 for v in head_rows]
        for mask in middle[::-1]:
            for which, tail in enumerate(tails):
                keep, give, offset = [], [], 0
                for size in sizes:
                    keep.append(tail[offset : offset + size // 2])
                    give.append(tail[offset + size // 2 : offset + size])
                    offset += size
                tails[which] = jnp.concatenate(keep) + swap(jnp.concatenate(give), mask)
            sizes = [size // 2 for size in sizes]
        for mask in middle:
            features = features + swap(features, mask)
        features, tails = after((features, tails), given[3])
        came = swap(jnp.concatenate([features, tails[1]]), top)
        features = features + swap(features, low) + swap(features, low | top)
        features = (features + came[:cut]).reshape(lines, depth)
        tail = tails[0] + came[cut:]
        ends = [sum(sizes[: i + 1]) for i in range(len(sizes))]
        grad_b_up, grad_b_query, grad_b_value = [
            tail[end - size : end].reshape(-1) for end, size in zip(ends, sizes)
        ]
        grad_w_down, grad_w_up = totals[0][0], totals[1][0]
        grad_w_out, grad_w_query = jnp.split(totals[2][0], 2, axis=1)
        grad_w_key, grad_w_value = jnp.split(totals[3][0], 2, axis=1)
        mean_loss = features[4, 0] / (valid_count * depth)
        return (
            to_absolute(narrow(output)),
            mean_loss,
            to_absolute(grad_tokens),
            features[5],
            features[6],
            grad_w_query,
            grad_b_query,
            grad_w_key,
            grad_w_value,
            grad_b_value,
            grad_w_out,
            features[2],
            features[0],
            features[1],
            grad_w_up,
            grad_b_up,
            grad_w_down,
            features[3],
        )

    return body


def solution(mesh):
    placed = (
        P(("fsdp", "tp"), None),
        P(),
        P(),
        P("fsdp", "tp"),
        P("tp"),
        P("fsdp", "tp"),
        P("fsdp", "tp"),
        P("tp"),
        P("fsdp", "tp"),
        P(),
        P(),
        P(),
        P("fsdp", "tp"),
        P("tp"),
        P("fsdp", "tp"),
        P(),
        P(("fsdp", "tp"), None),
        P(("fsdp", "tp")),
        P("fsdp", None),
        P("fsdp", None, None),
    )
    return jax.shard_map(
        make_body(mesh.shape["fsdp"], mesh.shape["tp"]),
        mesh=mesh,
        in_specs=placed,
        out_specs=(
            P(("fsdp", "tp"), None),
            P(),
            P(("fsdp", "tp"), None),
            P(),
            P(),
            P("fsdp", "tp"),
            P("tp"),
            P("fsdp", "tp"),
            P("fsdp", "tp"),
            P("tp"),
            P("fsdp", "tp"),
            P(),
            P(),
            P(),
            P("fsdp", "tp"),
            P("tp"),
            P("fsdp", "tp"),
            P(),
        ),
        check_vma=False,
    )
```
